32 devices in a mesh: probe: 16 (over z, y, core), strip: 2 (over x).
Axes of the slice: x: 2, y: 2, z: 4, core: 2. Of those that a mesh axis runs over, the one named last changes fastest.
Arguments:
- potential: float32 [2, 512, 2048], P(None, 'probe', 'strip'), may hold values from 0 to 2
- probe_wave: float32 [2, 256, 256], replicated, may hold values from -6 to 6
- offsets: int32 [2, 2, 96], P('strip'), may hold values from -128 to 896, as said below
- members: int32 [2, 16, 6], P('strip', 'probe'), may hold values from 0 to 95, as said below
- counts: int32 [2, 16], P('strip', 'probe'), may hold values from 1 to 6, as said below
- measured: float32 [2, 16, 6, 256, 256], P('strip', 'probe'), may hold values from 0 to 4
Outputs:
- potential_grad: float32 [2, 512, 2048], P(None, 'probe', 'strip')
The draws below stay inside these ranges and needn't reach their ends.
Inputs may be any that keep to these rules, and one draw needn't show every extreme that they name: offsets[s, 0, p] is a window's first row, 0 to 256; offsets[s, 1, p] its first column counted from the strip's first column, -128 to 896; both ends of both ranges occur in every strip. `members`: every position of a strip is listed exactly once over that strip's groups; a group uses its first counts[s, g] entries. `counts`: in every strip some group uses all 6 slots and some group uses one.
All inputs are finite; a program needn't handle non-finite values.
Results may differ from the reference program's by a relative error of at most 0.00021.
Values sent between devices are 32-bit elements; how exact they have to be, the bound alone decides.
No kernel may reach another device: no remote copies, remote signals or barrier semaphores. Data moves between devices by JAX's collectives and lax.ppermute only.
A program may use at most 64 MiB of HBM per device.

```python
import jax
import jax.numpy as jnp
from jax import lax

PW = 256
NSLICE = 2
SH = 512
SW = 1024
EDGE = 128
GMAX = 6
STRIPS = 2
GROUPS = 16
POS = 96
SW_ALL = 2048


def draw_offsets(key, part):
    first_key, second_key = jax.random.split(jax.random.fold_in(key, 11))
    rows_drawn = jax.random.randint(first_key, (STRIPS, POS), 0, SH - PW + 1)
    columns_drawn = jax.random.randint(second_key, (STRIPS, POS), -EDGE, SW + EDGE - PW + 1)
    rows_drawn = rows_drawn.at[:, 0].set(0).at[:, 1].set(SH - PW)
    columns_drawn = columns_drawn.at[:, 0].set(-EDGE).at[:, 1].set(SW + EDGE - PW)
    return jnp.stack([rows_drawn, columns_drawn], axis=1).astype(jnp.int32)


def draw_members(key, part):
    strip_keys = jax.random.split(jax.random.fold_in(key, 23), STRIPS)
    orders = jax.vmap(lambda one_key: jax.random.permutation(one_key, POS))(strip_keys)
    return orders.reshape(STRIPS, GROUPS, GMAX).astype(jnp.int32)


def draw_counts(key, part):
    first_key, second_key = jax.random.split(jax.random.fold_in(key, 37))
    drawn = jax.random.randint(first_key, (STRIPS, GROUPS), 1, GMAX + 1)
    full_group = jax.random.randint(second_key, (STRIPS,), 0, GROUPS)
    single_group = (full_group + 1) % GROUPS
    group_ids = jnp.arange(GROUPS)[None, :]
    drawn = jnp.where(group_ids == single_group[:, None], 1, drawn)
    drawn = jnp.where(group_ids == full_group[:, None], GMAX, drawn)
    return drawn.astype(jnp.int32)


def block_levels(own_key, dims, cuts, least, largest):
    def one(axis_at, blocks):
        heights = jax.random.uniform(jax.random.fold_in(jax.random.fold_in(own_key, 6), axis_at), (blocks,), jnp.float32, least / len(cuts), largest / len(cuts))
        return jnp.repeat(jnp.exp(heights), dims[axis_at] // blocks).reshape((-1,) + (1,) * (len(dims) - axis_at - 1))

    factor_of = one(*cuts[0])
    for cut in cuts[1:]:
        factor_of = factor_of * one(*cut)
    return factor_of


def centred(rng, extent, spread, reach, held_as=jnp.bfloat16):
    return jnp.clip(spread * jax.random.normal(rng, extent, jnp.float32), -reach, reach).astype(held_as)


def setup_inputs(seed: int = 0) -> dict:
    key_list = jax.random.split(jax.random.key(seed), 7)
    return {
        "potential": jnp.clip(2.0 * jax.random.uniform(key_list[0], (NSLICE, SH, SW_ALL), jnp.float32) ** block_levels(key_list[0], (NSLICE, SH, SW_ALL), ((1, 16), (2, 2)), -0.2, 0.2), 0.0, 2.0),
        "probe_wave": centred(key_list[1], (2, PW, PW), 1.0, 6.0, jnp.float32),
        "offsets": draw_offsets(jax.random.fold_in(key_list[6], 71), 0),
        "members": draw_members(jax.random.fold_in(key_list[6], 71), 0),
        "counts": draw_counts(jax.random.fold_in(key_list[6], 71), 0),
        "measured": jnp.clip(4.0 * jax.random.uniform(key_list[5], (STRIPS, GROUPS, GMAX, PW, PW), jnp.float32) ** block_levels(key_list[5], (STRIPS, GROUPS, GMAX, PW, PW), ((0, 2), (1, 16)), -0.2, 0.2), 0.0, 4.0),
    }


A_PROP = 0.1
LOSS_SCALE = 0.03125

def laplace(values):
    padded = jnp.pad(values, ((1, 1), (1, 1)))
    return padded[2:, 1:-1] + padded[:-2, 1:-1] + padded[1:-1, 2:] + padded[1:-1, :-2] - 4.0 * values

def propagate(real_part, imag_part):
    term_re, term_im = (real_part, imag_part)
    out_re, out_im = (real_part, imag_part)
    for degree in range(1, 5):
        lap_re = laplace(term_re)
        lap_im = laplace(term_im)
        term_re, term_im = (-A_PROP / degree * lap_im, A_PROP / degree * lap_re)
        out_re = out_re + term_re
        out_im = out_im + term_im
    return (out_re, out_im)

def exit_wave(window, probe_wave):
    real_part, imag_part = (probe_wave[0], probe_wave[1])
    for slice_index in range(window.shape[0]):
        phases = window[slice_index]
        cosine, sine_part = (jnp.cos(phases), jnp.sin(phases))
        real_part, imag_part = (real_part * cosine - imag_part * sine_part, real_part * sine_part + imag_part * cosine)
        real_part, imag_part = propagate(real_part, imag_part)
    return (real_part, imag_part)

def slot_loss(window, probe_wave, intensity_data):
    real_part, imag_part = exit_wave(window, probe_wave)
    far_wave = jnp.fft.fft2(real_part + 1j * imag_part, norm='ortho')
    intensity = jnp.real(far_wave) ** 2 + jnp.imag(far_wave) ** 2
    return LOSS_SCALE * jnp.sum((intensity - intensity_data) ** 2)

def reference(potential, probe_wave, offsets, members, counts, measured):
    padded = jnp.pad(potential, ((0, 0), (0, 0), (EDGE, EDGE)))
    anchor = jnp.zeros((), jnp.int32)

    def visit(item, gradient):
        strip_index = (item // (GROUPS * GMAX)).astype(jnp.int32)
        group_index = (item // GMAX % GROUPS).astype(jnp.int32)
        slot_index = (item % GMAX).astype(jnp.int32)
        position = members[strip_index, group_index, slot_index]
        start_row = offsets[strip_index, 0, position].astype(jnp.int32)
        start_column = (strip_index * SW + EDGE + offsets[strip_index, 1, position]).astype(jnp.int32)
        window = lax.dynamic_slice(padded, (anchor, start_row, start_column), (NSLICE, PW, PW))
        window_grad = jax.grad(slot_loss)(window, probe_wave, measured[strip_index, group_index, slot_index])
        weight = (slot_index < counts[strip_index, group_index]).astype(jnp.float32)
        current = lax.dynamic_slice(gradient, (anchor, start_row, start_column), (NSLICE, PW, PW))
        return lax.dynamic_update_slice(gradient, current + weight * window_grad, (anchor, start_row, start_column))
    gradient = lax.fori_loop(0, STRIPS * GROUPS * GMAX, visit, jnp.zeros(padded.shape, jnp.float32))
    return gradient[:, :, EDGE:EDGE + SW_ALL]
```

```python
import math

import jax
import jax.numpy as jnp
from jax import lax
from jax.experimental import pallas as pl
from jax.experimental.pallas import tpu as pltpu
from jax.sharding import PartitionSpec as P

EDGE = 128
A_PROP = 0.1
LOSS_SCALE = 0.03125
LANES = 128
SUB = 8
COS = (0.9999999993567104, -0.4999999690796125, 0.041666428711172335, -0.0013882473076505886, 2.4093931432702378e-05)
SIN = (0.9999999999413409, -0.1666666638472293, 0.008333311638477454, -0.00019835422091007726, 2.6912728384156356e-06)


def extended(value, sides, width):
    for axis, dim in sides:
        peers, length = (lax.axis_size(axis), value.shape[dim])
        up = [(i, (i + 1) % peers) for i in range(peers - 1)]
        down = [(j, i) for i, j in up]
        last = lax.slice_in_dim(value, length - width, length, axis=dim)
        initial = lax.slice_in_dim(value, 0, width, axis=dim)
        before = lax.ppermute(last, axis, up)
        after = lax.ppermute(initial, axis, down)
        value = jnp.concatenate([before, value, after], axis=dim)
    return value


def split(value):
    high = value.astype(jnp.bfloat16)
    return high, (value - high.astype(jnp.float32)).astype(jnp.bfloat16)


def split_table(value):
    high = lax.reduce_precision(value, 8, 7)
    return high.astype(jnp.bfloat16), (value - high).astype(jnp.bfloat16)


def tables(size):
    groups = size // SUB
    indices = jnp.arange(size, dtype=jnp.int32)
    order = indices % SUB * groups + indices // SUB

    def wave(rows, columns):
        angles = -2.0 * math.pi / size * (rows[:, None] * columns[None, :] % size).astype(jnp.float32)
        scale = 1.0 / math.sqrt(size)
        return jnp.cos(angles) * scale, jnp.sin(angles) * scale

    def left(real, imag):
        full = jnp.concatenate([jnp.concatenate([real, -imag], 1), jnp.concatenate([imag, real], 1)], 0)
        high, low = split_table(full)
        return jnp.concatenate([high, high, low], 1)

    def right(real, imag):
        full = jnp.concatenate([jnp.concatenate([real, imag], 1), jnp.concatenate([-imag, real], 1)], 0)
        high, low = split_table(full)
        return jnp.concatenate([high, high, low], 0)

    forward = wave(indices, order)
    backward = wave(order, indices)
    return left(*forward), left(*backward), right(*wave(indices, indices))


def kernel(
    rows_ref, columns_ref, count_ref,
    object_ref, probe_ref, measured_ref, left_ref, left_back_ref, right_ref,
    out_ref,
    base, ping, pong, first, second, turn, stack, wide,
    *, height, blocks, slices,
):
    slot = pl.program_id(0)
    size = measured_ref.shape[-1]
    groups = size // SUB
    halves = size // LANES
    per_block = blocks * slices * height
    stride = groups // height * per_block
    lane = lax.broadcasted_iota(jnp.int32, (SUB, LANES), 1)
    sub = lax.broadcasted_iota(jnp.int32, (SUB, LANES), 0)

    @pl.when(slot == 0)
    def _():
        def clear(i, carry):
            out_ref[pl.ds(pl.multiple_of(i * LANES, LANES), LANES), :] = jnp.zeros((LANES, LANES), jnp.float32)
            return carry
        lax.fori_loop(0, out_ref.shape[0] // LANES, clear, 0)

    @pl.when(slot < count_ref[0])
    def _():
        start_row = rows_ref[slot]
        start_column = columns_ref[slot]
        block = start_column // LANES
        shift = start_column % LANES
        back = lax.rem(LANES - shift, LANES)
        places = [jnp.minimum(block + k, blocks - 1) * (slices * height) for k in range(halves + 1)]
        keep = lane < LANES - shift
        spill = lane < shift

        def object_rows(t, j):
            at = start_row + t
            return at // height * per_block + j * height + at % height

        def window(t, j):
            top = object_rows(t, j)
            parts = [pltpu.roll(object_ref[pl.ds(top + c, SUB, stride=stride), :], back, 1) for c in places]
            return [jnp.where(keep, parts[k], parts[k + 1]) for k in range(halves)]

        def phase(t, j):
            out = []
            for value in window(t, j):
                theta = value - 1.0
                z = theta * theta
                c = COS[4]
                s = SIN[4]
                for k in (3, 2, 1, 0):
                    c = c * z + COS[k]
                    s = s * z + SIN[k]
                out.append((c, s * theta))
            return out

        def tile(t):
            return pl.ds(pl.multiple_of((t + 1) * SUB, SUB), SUB)

        def half(h):
            return pl.ds(h * LANES, LANES)

        def halo(ref):
            for part in range(2):
                for h in range(halves):
                    bottom = ref[part, tile(groups - 1), half(h)]
                    top = ref[part, tile(0), half(h)]
                    ref[part, tile(-1), half(h)] = jnp.where(sub == 0, 0.0, pltpu.roll(bottom, 1, 0))
                    ref[part, tile(groups), half(h)] = jnp.where(sub == SUB - 1, 0.0, pltpu.roll(top, SUB - 1, 0))

        def laplace(ref, part, t):
            out = []
            middle = [ref[part, tile(t), half(h)] for h in range(halves)]
            right_rolled = [pltpu.roll(v, 1, 1) for v in middle]
            left_rolled = [pltpu.roll(v, LANES - 1, 1) for v in middle]
            for h in range(halves):
                before = jnp.where(lane == 0, right_rolled[h - 1] if h else 0.0, right_rolled[h])
                after = jnp.where(lane == LANES - 1, left_rolled[h + 1] if h + 1 < halves else 0.0, left_rolled[h])
                around = (before + after) + (ref[part, tile(t - 1), half(h)] + ref[part, tile(t + 1), half(h)])
                out.append(around - 4.0 * middle[h])
            return out

        def step(src, dst, factor):
            def body(i, carry):
                for d in range(4):
                    t = i * 4 + d
                    lap_re = laplace(src, 0, t)
                    lap_im = laplace(src, 1, t)
                    for h in range(halves):
                        dst[0, tile(t), half(h)] = base[0, tile(t), half(h)] - factor * lap_im[h]
                        dst[1, tile(t), half(h)] = base[1, tile(t), half(h)] + factor * lap_re[h]
                return carry
            lax.fori_loop(0, groups // 4, body, 0)

        def propagate():
            halo(base)
            step(base, ping, A_PROP / 4)
            halo(ping)
            step(ping, pong, A_PROP / 3)
            halo(pong)
            step(pong, ping, A_PROP / 2)
            halo(ping)
            step(ping, pong, A_PROP)

        def each(body):
            def run(i, carry):
                for d in range(4):
                    body(i * 4 + d)
                return carry
            lax.fori_loop(0, groups // 4, run, 0)

        def enter_first(t):
            for h, (c, s) in enumerate(phase(t, 0)):
                re = probe_ref[pl.ds(h * size + t, SUB, stride=groups), :]
                im = probe_ref[pl.ds((halves + h) * size + t, SUB, stride=groups), :]
                new_re, new_im = re * c - im * s, re * s + im * c
                base[0, tile(t), half(h)] = new_re
                base[1, tile(t), half(h)] = new_im
                first[0, tile(t), half(h)] = new_re
                first[1, tile(t), half(h)] = new_im

        def enter_second(t):
            for h, (c, s) in enumerate(phase(t, 1)):
                re = pong[0, tile(t), half(h)]
                im = pong[1, tile(t), half(h)]
                new_re, new_im = re * c - im * s, re * s + im * c
                base[0, tile(t), half(h)] = new_re
                base[1, tile(t), half(h)] = new_im
                second[0, tile(t), half(h)] = new_re
                second[1, tile(t), half(h)] = new_im
                turn[0, tile(t), half(h)] = c
                turn[1, tile(t), half(h)] = s

        def add_gradient(t, j, grads):
            top = object_rows(t, j)
            rolled = [pltpu.roll(g, shift, 1) for g in grads]
            for k, c in enumerate(places):
                here = jnp.where(spill, rolled[k - 1] if k else 0.0, rolled[k] if k < halves else 0.0)
                rows = pl.ds(top + c, SUB, stride=stride)
                out_ref[rows, :] = out_ref[rows, :] + here

        def leave_second(t):
            grads = []
            for h in range(halves):
                re = pong[0, tile(t), half(h)]
                im = pong[1, tile(t), half(h)]
                grads.append(-(re * second[1, tile(t), half(h)] + im * second[0, tile(t), half(h)]))
                c = turn[0, tile(t), half(h)]
                s = turn[1, tile(t), half(h)]
                base[0, tile(t), half(h)] = re * c - im * s
                base[1, tile(t), half(h)] = re * s + im * c
            add_gradient(t, 1, grads)

        def leave_first(t):
            grads = []
            for h in range(halves):
                re = pong[0, tile(t), half(h)]
                im = pong[1, tile(t), half(h)]
                grads.append(-(re * first[1, tile(t), half(h)] + im * first[0, tile(t), half(h)]))
            add_gradient(t, 0, grads)

        def dot(a, b):
            return jnp.dot(a, b, preferred_element_type=jnp.float32)

        def put_wide(real, imag):
            for k, value in enumerate((real, imag)):
                high, low = split(value)
                for place, piece in ((k, high), (2 + k, low), (4 + k, high)):
                    wide[:, place * size:(place + 1) * size] = piece

        each(enter_first)
        propagate()
        each(enter_second)
        propagate()
        for part in range(2):
            high, low = split(pong[part, SUB:SUB + size, :])
            for place, piece in ((part, high), (2 + part, low), (4 + part, high)):
                stack[place * size:(place + 1) * size, :] = piece
        inner = dot(left_ref[...], stack[...])
        put_wide(inner[:size], inner[size:])
        far = dot(wide[...], right_ref[...])
        far_re, far_im = far[:, :size], far[:, size:]
        scaled = (4.0 * LOSS_SCALE) * ((far_re * far_re + far_im * far_im) - measured_ref[...])
        put_wide(scaled * far_re, -(scaled * far_im))
        inner = dot(wide[...], right_ref[...])
        for part in range(2):
            high, low = split(inner[:, part * size:(part + 1) * size])
            for place, piece in ((part, high), (2 + part, low), (4 + part, high)):
                stack[place * size:(place + 1) * size, :] = piece
        outer = dot(left_back_ref[...], stack[...])
        base[0, SUB:SUB + size, :] = outer[:size]
        base[1, SUB:SUB + size, :] = outer[size:]
        propagate()
        each(leave_second)
        propagate()
        each(leave_first)


def window_gradients(rows, columns, count, whole, probe, measured, height, slices):
    size = measured.shape[-1]
    slots = measured.shape[0]
    padded = size + 2 * SUB
    blocks = whole.shape[1] // (slices * height)
    peers = whole.shape[0]
    whole = whole.reshape(-1, LANES)
    left, left_back, right = tables(size)
    full = lambda a: pl.BlockSpec(a.shape, lambda k, *_: (0,) * a.ndim)
    field = pltpu.VMEM((2, padded, size), jnp.float32)
    return pl.pallas_call(
        lambda *refs: kernel(*refs, height=height, blocks=blocks, slices=slices),
        grid_spec=pltpu.PrefetchScalarGridSpec(
            num_scalar_prefetch=3,
            grid=(slots,),
            in_specs=[
                full(whole), full(probe),
                pl.BlockSpec((None, size, size), lambda k, *_: (k, 0, 0)),
                full(left), full(left_back), full(right),
            ],
            out_specs=pl.BlockSpec(whole.shape, lambda k, *_: (0, 0)),
            scratch_shapes=[field] * 6 + [
                pltpu.VMEM((6 * size, size), jnp.bfloat16),
                pltpu.VMEM((size, 6 * size), jnp.bfloat16),
            ],
        ),
        out_shape=jax.ShapeDtypeStruct(whole.shape, jnp.float32),
        compiler_params=pltpu.CompilerParams(vmem_limit_bytes=56 * 2**20),
        name="windows",
    )(rows, columns, count, whole, probe, measured, left, left_back, right)


def to_blocks(value):
    slices, height, width = value.shape
    return value.reshape(slices * height, width // LANES, LANES).transpose(1, 0, 2)


def from_blocks(value, slices):
    blocks, rows, lanes = value.shape
    return value.transpose(1, 0, 2).reshape(slices, rows // slices, blocks * lanes)


def shards(potential, probe_wave, offsets, members, counts, measured):
    slices, height, own_width = potential.shape
    size = probe_wave.shape[-1]
    strips = lax.axis_size("strip")
    up = [(i, i + 1) for i in range(strips - 1)]
    down = [(j, i) for i, j in up]
    own = to_blocks(potential)
    edge = EDGE // LANES
    from_left = lax.ppermute(own[-edge:], "strip", up)
    from_right = lax.ppermute(own[:edge], "strip", down)
    widened = jnp.concatenate([from_left, own, from_right], 0).reshape(-1, LANES)
    gathered = lax.all_gather(widened, "probe", axis=0, tiled=False)
    positions = members[0, 0]
    rows = offsets[0, 0][positions]
    columns = offsets[0, 1][positions] + EDGE
    probe = probe_wave.reshape(2 * size, size // LANES, LANES)
    probe = probe.reshape(2, size, size // LANES, LANES).transpose(0, 2, 1, 3).reshape(-1, LANES)
    gradient = window_gradients(rows, columns, counts[0], gathered, probe, measured[0, 0], height, slices)
    mine = lax.psum_scatter(gradient.reshape(gathered.shape), "probe", scatter_dimension=0, tiled=False)
    mine = mine.reshape(-1, slices * height, LANES)
    from_left = lax.ppermute(mine[-edge:], "strip", up)
    from_right = lax.ppermute(mine[:edge], "strip", down)
    middle = mine[edge:-edge]
    middle = middle.at[:edge].add(from_left).at[-edge:].add(from_right)
    return from_blocks(middle, slices)


def solution(mesh):
    placed = (
        P(None, "probe", "strip"),
        P(),
        P("strip", None, None),
        P("strip", "probe", None),
        P("strip", "probe"),
        P("strip", "probe", None, None, None),
    )
    return jax.shard_map(
        shards, mesh=mesh, in_specs=placed, out_specs=P(None, "probe", "strip"), check_vma=False
    )
```

```python
import math

import jax
import jax.numpy as jnp
from jax import lax
from jax.experimental import pallas as pl
from jax.experimental.pallas import tpu as pltpu
from jax.sharding import PartitionSpec as P

EDGE = 128
A_PROP = 0.1
LOSS_SCALE = 0.03125
LANES = 128
SUB = 8
COS = (0.9999999993567104, -0.4999999690796125, 0.041666428711172335, -0.0013882473076505886, 2.4093931432702378e-05)
SIN = (0.9999999999413409, -0.1666666638472293, 0.008333311638477454, -0.00019835422091007726, 2.6912728384156356e-06)


def split(value):
    high = value.astype(jnp.bfloat16)
    return high, (value - high.astype(jnp.float32)).astype(jnp.bfloat16)


def split_table(value):
    high = lax.reduce_precision(value, 8, 7)
    return high.astype(jnp.bfloat16), (value - high).astype(jnp.bfloat16)


def tables(size):
    half = jnp.arange(size // 2, dtype=jnp.int32)

    def wave(exponents):
        angles = -2.0 * math.pi / size * (exponents % size).astype(jnp.float32)
        scale = 1.0 / math.sqrt(size)
        return jnp.cos(angles) * scale, jnp.sin(angles) * scale

    def left(real, imag):
        high, low = split_table(jnp.block([[real, -imag], [imag, real]]))
        return jnp.concatenate([high, high, low], 1)

    def right(real, imag):
        high, low = split_table(jnp.block([[real, imag], [-imag, real]]))
        return jnp.concatenate([high, high, low], 0)

    even = wave(2 * half[:, None] * half[None, :])
    odd = wave((2 * half[:, None] + 1) * half[None, :])
    odd_back = wave(half[:, None] * (2 * half[None, :] + 1))
    return left(*even), left(*odd), left(*odd_back), right(*even), right(*odd), right(*odd_back)


def parity(width):
    columns = lax.broadcasted_iota(jnp.int32, (width, width), 1)
    rows = lax.broadcasted_iota(jnp.int32, (width, width), 0)
    source = columns % (width // 2) * 2 + columns // (width // 2)
    return (rows == source).astype(jnp.float32).astype(jnp.bfloat16)


def exact_dot(value, selection):
    high = value.astype(jnp.bfloat16)
    rest = value - high.astype(jnp.float32)
    middle = rest.astype(jnp.bfloat16)
    low = (rest - middle.astype(jnp.float32)).astype(jnp.bfloat16)
    total = jnp.dot(high, selection, preferred_element_type=jnp.float32)
    total = total + jnp.dot(middle, selection, preferred_element_type=jnp.float32)
    return total + jnp.dot(low, selection, preferred_element_type=jnp.float32)


def deal_kernel(x_ref, o_ref):
    pair = 2 * LANES
    selection = parity(pair)
    for k in range(x_ref.shape[1] // pair):
        dealt = exact_dot(x_ref[:, k * pair:(k + 1) * pair], selection)
        for p in range(2):
            o_ref[p, k] = dealt[:, p * LANES:(p + 1) * LANES]


def deal(value):
    rows, width = value.shape
    return pl.pallas_call(
        deal_kernel,
        out_shape=jax.ShapeDtypeStruct((2, width // (2 * LANES), rows, LANES), jnp.float32),
        name="deal",
    )(value)


def weave_kernel(x_ref, left_ref, right_ref, o_ref):
    pair = 2 * LANES
    rows = lax.broadcasted_iota(jnp.int32, (pair, pair), 0)
    columns = lax.broadcasted_iota(jnp.int32, (pair, pair), 1)
    selection = (columns == rows % LANES * 2 + rows // LANES).astype(jnp.float32).astype(jnp.bfloat16)
    lane = lax.broadcasted_iota(jnp.int32, o_ref.shape[:1] + (LANES,), 1)
    blocks = o_ref.shape[1] // pair
    for k in range(blocks):
        parts = []
        for p in range(2):
            value = x_ref[p, k]
            if k == 0:
                value = value + jnp.where(lane < EDGE // 2, left_ref[p], 0.0)
            if k == blocks - 1:
                value = value + jnp.where(lane >= LANES - EDGE // 2, right_ref[p], 0.0)
            parts.append(value)
        o_ref[:, k * pair:(k + 1) * pair] = exact_dot(jnp.concatenate(parts, 1), selection)


def weave(value, from_left, from_right):
    _, blocks, rows, _ = value.shape
    return pl.pallas_call(
        weave_kernel,
        out_shape=jax.ShapeDtypeStruct((rows, (blocks - 1) * 2 * LANES), jnp.float32),
        name="weave",
    )(value, from_left, from_right)


def kernel(
    rows_ref, columns_ref, count_ref,
    pieces_ref, probe_ref, low_ref, high_ref,
    left_even, left_odd, left_odd_back, right_even, right_odd, right_odd_back,
    out_ref,
    whole, total, base, ping, pong, first, second, turn, stack_even, stack_odd, wide_even, wide_odd, sems,
    *, blocks, slices,
):
    slot = pl.program_id(0)
    size = low_ref.shape[0]
    half = size // 2
    groups = size // SUB
    peers = pieces_ref.shape[0]
    height = pieces_ref.shape[2]
    lane = lax.broadcasted_iota(jnp.int32, (SUB, LANES), 1)

    def rows_of(device):
        return pl.ds(device * height, height)

    @pl.when(slot == 0)
    def _():
        copies = [
            pltpu.make_async_copy(pieces_ref.at[d], whole.at[:, rows_of(d), :], sems.at[0]) for d in range(peers)
        ]
        for copy in copies:
            copy.start()

        def clear(i, carry):
            for k in range(total.shape[0]):
                total[k, pl.ds(pl.multiple_of(i * SUB, SUB), SUB), :] = jnp.zeros((SUB, LANES), jnp.float32)
            return carry
        lax.fori_loop(0, total.shape[1] // SUB, clear, 0)
        for field in (base, ping, pong):
            for part in range(2):
                for p in range(2):
                    field[part, p, :SUB] = jnp.zeros((SUB, LANES), jnp.float32)
                    field[part, p, SUB + size:] = jnp.zeros((SUB, LANES), jnp.float32)
        for copy in copies:
            copy.wait()

    @pl.when(slot < count_ref[0])
    def _():
        start_row = rows_ref[slot]
        start_column = columns_ref[slot]
        sources = []
        for p in range(2):
            column = start_column + p
            at = (column + blocks * 2 * LANES) // 2
            side = lax.rem(column + blocks * 2 * LANES, 2)
            block = lax.rem(at // LANES, blocks)
            after = lax.rem(at // LANES + 1, blocks)
            sources.append((side * blocks + block, side * blocks + after, at % LANES))

        def tile(t):
            return slice(SUB + t * SUB, 2 * SUB + t * SUB)

        def window(t, j):
            rows = pl.ds(start_row + t * SUB, SUB)
            out = []
            for block, after, shift in sources:
                back = lax.rem(LANES - shift, LANES)
                here = pltpu.roll(whole[block * slices + j, rows, :], back, 1)
                there = pltpu.roll(whole[after * slices + j, rows, :], back, 1)
                out.append(jnp.where(lane < LANES - shift, here, there))
            return out

        def phase(t, j):
            out = []
            for value in window(t, j):
                theta = value - 1.0
                z = theta * theta
                c = COS[4]
                s = SIN[4]
                for k in (3, 2, 1, 0):
                    c = c * z + COS[k]
                    s = s * z + SIN[k]
                out.append((c, s * theta))
            return out

        def laplace(ref, part, t):
            even, odd = (ref[part, p, tile(t)] for p in range(2))
            row = SUB + t * SUB
            even_rows = ref[part, 0, row - 1:row + SUB - 1] + ref[part, 0, row + 1:row + SUB + 1]
            odd_rows = ref[part, 1, row - 1:row + SUB - 1] + ref[part, 1, row + 1:row + SUB + 1]
            even_columns = odd + jnp.where(lane == 0, 0.0, pltpu.roll(odd, 1, 1))
            odd_columns = even + jnp.where(lane == LANES - 1, 0.0, pltpu.roll(even, LANES - 1, 1))
            return (even_rows + even_columns) - 4.0 * even, (odd_rows + odd_columns) - 4.0 * odd

        def step(src, dst, factor):
            for t in range(groups):
                lap_re = laplace(src, 0, t)
                lap_im = laplace(src, 1, t)
                for p in range(2):
                    dst[0, p, tile(t)] = base[0, p, tile(t)] - factor * lap_im[p]
                    dst[1, p, tile(t)] = base[1, p, tile(t)] + factor * lap_re[p]

        def propagate():
            step(base, ping, A_PROP / 4)
            step(ping, pong, A_PROP / 3)
            step(pong, ping, A_PROP / 2)
            step(ping, pong, A_PROP)

        def enter(t, j, source, offset, kept):
            for p, (c, s) in enumerate(phase(t, j)):
                re = source[0, p, pl.ds(offset + t * SUB, SUB)]
                im = source[1, p, pl.ds(offset + t * SUB, SUB)]
                new_re, new_im = re * c - im * s, re * s + im * c
                base[0, p, tile(t)] = new_re
                base[1, p, tile(t)] = new_im
                kept[0, p, tile(t)] = new_re
                kept[1, p, tile(t)] = new_im
                if j == slices - 1:
                    turn[0, p, tile(t)] = c
                    turn[1, p, tile(t)] = s

        def leave(t, j, kept):
            rows = pl.ds(start_row + t * SUB, SUB)
            for p, (block, after, shift) in enumerate(sources):
                re = pong[0, p, tile(t)]
                im = pong[1, p, tile(t)]
                grad = -(re * kept[1, p, tile(t)] + im * kept[0, p, tile(t)])
                if j:
                    c = turn[0, p, tile(t)]
                    s = turn[1, p, tile(t)]
                    base[0, p, tile(t)] = re * c - im * s
                    base[1, p, tile(t)] = re * s + im * c
                rolled = pltpu.roll(grad, shift, 1)
                here = block * slices + j
                there = after * slices + j
                total[here, rows, :] = total[here, rows, :] + jnp.where(lane < shift, 0.0, rolled)
                total[there, rows, :] = total[there, rows, :] + jnp.where(lane < shift, rolled, 0.0)

        def dot(a, b):
            return jnp.dot(a[...], b[...], preferred_element_type=jnp.float32)

        def put_stack(stack, part, p, value):
            high, low = split(value)
            for k, piece in enumerate((high, low, high)):
                stack[k * size + part * half:k * size + (part + 1) * half, p * LANES:(p + 1) * LANES] = piece

        def put_wide(wide, rows, part, value):
            high, low = split(value)
            for k, piece in enumerate((high, low, high)):
                wide[rows, k * size + part * half:k * size + (part + 1) * half] = piece

        def lanes(k):
            return slice(k * LANES, (k + 1) * LANES)

        for t in range(groups):
            enter(t, 0, probe_ref, 0, first)
        propagate()
        for t in range(groups):
            enter(t, 1, pong, SUB, second)
        propagate()

        upper, lower = slice(0, half), slice(half, size)
        for part in range(2):
            for p in range(2):
                top = pong[part, p, SUB:SUB + half]
                bottom = pong[part, p, SUB + half:SUB + size]
                put_stack(stack_even, part, p, top + bottom)
                put_stack(stack_odd, part, p, top - bottom)
        for rows, inner in ((upper, dot(left_even, stack_even)), (lower, dot(left_odd, stack_odd))):
            for part, own in enumerate((upper, lower)):
                put_wide(wide_even, rows, part, inner[own, lanes(0)])
                put_wide(wide_odd, rows, part, inner[own, lanes(1)])
        even = dot(wide_even, right_even)
        odd = dot(wide_odd, right_odd)
        for k, rows in enumerate((upper, lower)):
            pulled = []
            for sign, data in ((1, low_ref), (-1, high_ref)):
                far_re = even[rows, lanes(0)] + sign * odd[rows, lanes(0)]
                far_im = even[rows, lanes(1)] + sign * odd[rows, lanes(1)]
                excess = (far_re * far_re + far_im * far_im) - data[pl.ds(k, half, stride=2), :]
                scaled = (4.0 * LOSS_SCALE) * excess
                pulled.append((scaled * far_re, -(scaled * far_im)))
            for part in range(2):
                put_wide(wide_even, rows, part, pulled[0][part] + pulled[1][part])
                put_wide(wide_odd, rows, part, pulled[0][part] - pulled[1][part])
        for p, inner in enumerate((dot(wide_even, right_even), dot(wide_odd, right_odd_back))):
            for part in range(2):
                put_stack(stack_even, part, p, inner[upper, lanes(part)])
                put_stack(stack_odd, part, p, inner[lower, lanes(part)])
        even = dot(left_even, stack_even)
        odd = dot(left_odd_back, stack_odd)
        for part, own in enumerate((upper, lower)):
            for p in range(2):
                base[part, p, SUB:SUB + half] = even[own, lanes(p)] + odd[own, lanes(p)]
                base[part, p, SUB + half:SUB + size] = even[own, lanes(p)] - odd[own, lanes(p)]

        propagate()
        for t in range(groups):
            leave(t, 1, second)
        propagate()
        for t in range(groups):
            leave(t, 0, first)

    @pl.when(slot == pl.num_programs(0) - 1)
    def _():
        copies = [
            pltpu.make_async_copy(total.at[:, rows_of(d), :], out_ref.at[d], sems.at[0]) for d in range(peers)
        ]
        for copy in copies:
            copy.start()
        for copy in copies:
            copy.wait()


def window_gradients(rows, columns, count, pieces, probe, measured, slices):
    slots, size = measured.shape[:2]
    peers, planes, height, _ = pieces.shape
    blocks = planes // (2 * slices)
    factors = tables(size)
    full = lambda a: pl.BlockSpec(a.shape, lambda k, *_: (0,) * a.ndim)
    field = pltpu.VMEM((2, 2, size + 2 * SUB, LANES), jnp.float32)
    plane = pltpu.VMEM((planes, peers * height, LANES), jnp.float32)
    tall = pltpu.VMEM((3 * size, size), jnp.bfloat16)
    wide = pltpu.VMEM((size, 3 * size), jnp.bfloat16)
    return pl.pallas_call(
        lambda *refs: kernel(*refs, blocks=blocks, slices=slices),
        grid_spec=pltpu.PrefetchScalarGridSpec(
            num_scalar_prefetch=3,
            grid=(slots,),
            in_specs=[
                pl.BlockSpec(memory_space=pl.ANY), full(probe),
                pl.BlockSpec((None, size, LANES), lambda k, *_: (k, 0, 0)),
                pl.BlockSpec((None, size, LANES), lambda k, *_: (k, 0, 1)),
                *[full(f) for f in factors],
            ],
            out_specs=pl.BlockSpec(memory_space=pl.ANY),
            scratch_shapes=[plane, plane] + [field] * 6 + [tall, tall, wide, wide, pltpu.SemaphoreType.DMA((1,))],
        ),
        out_shape=jax.ShapeDtypeStruct(pieces.shape, jnp.float32),
        compiler_params=pltpu.CompilerParams(vmem_limit_bytes=48 * 2**20),
        name="windows",
    )(rows, columns, count, pieces, probe, measured, measured, *factors)


def shards(potential, probe_wave, offsets, members, counts, measured):
    slices, height, own_width = potential.shape
    size = probe_wave.shape[-1]
    strips = lax.axis_size("strip")
    up = [(i, i + 1) for i in range(strips - 1)]
    down = [(j, i) for i, j in up]
    own = deal(potential.reshape(slices * height, own_width))
    from_left = lax.ppermute(own[:, -1], "strip", up)
    from_right = lax.ppermute(own[:, 0], "strip", down)
    lane = lax.broadcasted_iota(jnp.int32, from_left.shape, 2)
    edges = jnp.where(lane < EDGE // 2, from_right, from_left)
    piece = jnp.concatenate([own, edges[:, None]], 1)
    blocks = piece.shape[1]
    gathered = lax.all_gather(piece.reshape(-1, LANES), "probe", axis=0, tiled=False)
    positions = members[0, 0]
    rows = offsets[0, 0][positions]
    columns = offsets[0, 1][positions]
    probe = deal(probe_wave.reshape(2 * size, size)).reshape(2, 2, size, LANES).transpose(1, 0, 2, 3)
    gradient = window_gradients(
        rows, columns, counts[0], gathered.reshape(-1, 2 * blocks * slices, height, LANES), probe, measured[0, 0], slices
    )
    mine = lax.psum_scatter(gradient.reshape(gathered.shape), "probe", scatter_dimension=0, tiled=False)
    mine = mine.reshape(2, blocks, slices * height, LANES)
    from_left = lax.ppermute(mine[:, -1], "strip", up)
    from_right = lax.ppermute(mine[:, -1], "strip", down)
    return weave(mine, from_left, from_right).reshape(potential.shape)


def solution(mesh):
    placed = (
        P(None, "probe", "strip"),
        P(),
        P("strip", None, None),
        P("strip", "probe", None),
        P("strip", "probe"),
        P("strip", "probe", None, None, None),
    )
    return jax.shard_map(
        shards, mesh=mesh, in_specs=placed, out_specs=P(None, "probe", "strip"), check_vma=False
    )
```

```python
import functools
import math

import jax
import jax.numpy as jnp
from jax import lax
from jax.experimental import pallas as pl
from jax.experimental.pallas import tpu as pltpu
from jax.sharding import PartitionSpec as P

EDGE = 128
A_PROP = 0.1
LOSS_SCALE = 0.03125
LANES = 128
SUB = 8
COS = (0.9999999993567104, -0.4999999690796125, 0.041666428711172335, -0.0013882473076505886, 2.4093931432702378e-05)
SIN = (0.9999999999413409, -0.1666666638472293, 0.008333311638477454, -0.00019835422091007726, 2.6912728384156356e-06)


def split(value):
    high = value.astype(jnp.bfloat16)
    return high, (value - high.astype(jnp.float32)).astype(jnp.bfloat16)


def split_table(value):
    high = lax.reduce_precision(value, 8, 7)
    return high.astype(jnp.bfloat16), (value - high).astype(jnp.bfloat16)


def tables(size, zero):
    half = jnp.arange(size // 2, dtype=jnp.int32) + zero

    def wave(exponents):
        angles = -2.0 * math.pi / size * (exponents % size).astype(jnp.float32)
        scale = 1.0 / math.sqrt(size)
        return jnp.cos(angles) * scale, jnp.sin(angles) * scale

    def left(real, imag):
        high, low = split_table(jnp.block([[real, -imag], [imag, real]]))
        return jnp.concatenate([high, high, low], 1)

    def right(real, imag):
        high, low = split_table(jnp.block([[real, imag], [-imag, real]]))
        return jnp.concatenate([high, high, low], 0)

    even = wave(2 * half[:, None] * half[None, :])
    odd = wave((2 * half[:, None] + 1) * half[None, :])
    odd_back = wave(half[:, None] * (2 * half[None, :] + 1))
    return left(*even), left(*odd), left(*odd_back), right(*even), right(*odd), right(*odd_back)


def parity(width):
    columns = lax.broadcasted_iota(jnp.int32, (width, width), 1)
    rows = lax.broadcasted_iota(jnp.int32, (width, width), 0)
    source = columns % (width // 2) * 2 + columns // (width // 2)
    return (rows == source).astype(jnp.float32).astype(jnp.bfloat16)


def exact_dot(value, selection):
    high = value.astype(jnp.bfloat16)
    rest = value - high.astype(jnp.float32)
    middle = rest.astype(jnp.bfloat16)
    low = (rest - middle.astype(jnp.float32)).astype(jnp.bfloat16)
    total = jnp.dot(high, selection, preferred_element_type=jnp.float32)
    total = total + jnp.dot(middle, selection, preferred_element_type=jnp.float32)
    return total + jnp.dot(low, selection, preferred_element_type=jnp.float32)


def deal_kernel(*refs):
    *sources, o_ref = refs
    pair = 2 * LANES
    selection = parity(pair)
    at = 0
    for block in range(o_ref.shape[1]):
        if at < sources[0].shape[1]:
            value = sources[0][:, at:at + pair]
        else:
            value = jnp.concatenate([ref[...] for ref in sources[1:]], 1)
        at += pair
        dealt = exact_dot(value, selection)
        for p in range(2):
            o_ref[p, block] = dealt[:, p * LANES:(p + 1) * LANES]


def deal(value, *edges):
    rows, width = value.shape
    blocks = (width + sum(e.shape[1] for e in edges)) // (2 * LANES)
    return pl.pallas_call(
        deal_kernel,
        out_shape=jax.ShapeDtypeStruct((2, blocks, rows, LANES), jnp.float32),
        name="deal",
    )(value, *edges)


def weave_kernel(*refs):
    *terms, left_ref, right_ref, o_ref = refs
    pair = 2 * LANES
    rows = lax.broadcasted_iota(jnp.int32, (pair, pair), 0)
    columns = lax.broadcasted_iota(jnp.int32, (pair, pair), 1)
    selection = (columns == rows % LANES * 2 + rows // LANES).astype(jnp.float32).astype(jnp.bfloat16)
    lane = lax.broadcasted_iota(jnp.int32, o_ref.shape[:1] + (LANES,), 1)
    blocks = o_ref.shape[1] // pair
    for k in range(blocks):
        parts = []
        for p in range(2):
            value = terms[0][p, k]
            for term in terms[1:]:
                value = value + term[p, k]
            if k == 0:
                value = value + jnp.where(lane < EDGE // 2, left_ref[p], 0.0)
            if k == blocks - 1:
                value = value + jnp.where(lane >= LANES - EDGE // 2, right_ref[p], 0.0)
            parts.append(value)
        o_ref[:, k * pair:(k + 1) * pair] = exact_dot(jnp.concatenate(parts, 1), selection)


def weave(terms, from_left, from_right):
    _, blocks, rows, _ = terms[0].shape
    return pl.pallas_call(
        weave_kernel,
        out_shape=jax.ShapeDtypeStruct((rows, (blocks - 1) * 2 * LANES), jnp.float32),
        name="weave",
    )(*terms, from_left, from_right)


def kernel(
    rows_ref, columns_ref, count_ref,
    place_ref, probe_ref, low_ref, high_ref,
    left_even, left_odd, left_odd_back, right_even, right_odd, right_odd_back,
    pieces, outs,
    whole, total, base, ping, pong, first, second, turn, stack_even, stack_odd, wide_even, wide_odd, sems,
    *, blocks, slices, grid,
):
    slot = pl.program_id(0)
    size = low_ref.shape[0]
    half = size // 2
    groups = size // SUB
    height = pieces[0].shape[1]
    offsets = [(a, b, c) for a in range(grid[0]) for b in range(grid[1]) for c in range(grid[2])]
    lane = lax.broadcasted_iota(jnp.int32, (SUB, LANES), 1)

    def rows_of(offset, sign):
        device = 0
        for axis, count in enumerate(grid):
            device = device * count + lax.rem(place_ref[axis] + sign * offset[axis] + count, count)
        return pl.ds(pl.multiple_of(device * height, height), height)

    @pl.when(slot == 0)
    def _():
        copies = [
            pltpu.make_async_copy(piece, whole.at[:, rows_of(offset, -1), :], sems.at[0])
            for piece, offset in zip(pieces, offsets)
        ]
        for copy in copies:
            copy.start()

        def clear(i, carry):
            for k in range(total.shape[0]):
                total[k, pl.ds(pl.multiple_of(i * SUB, SUB), SUB), :] = jnp.zeros((SUB, LANES), jnp.float32)
            return carry
        lax.fori_loop(0, total.shape[1] // SUB, clear, 0)
        for field in (base, ping, pong):
            for part in range(2):
                for p in range(2):
                    field[part, p, :SUB] = jnp.zeros((SUB, LANES), jnp.float32)
                    field[part, p, SUB + size:] = jnp.zeros((SUB, LANES), jnp.float32)
        for copy in copies:
            copy.wait()

    @pl.when(slot < count_ref[0])
    def _():
        start_row = rows_ref[slot]
        start_column = columns_ref[slot]
        sources = []
        for p in range(2):
            column = start_column + p
            at = (column + blocks * 2 * LANES) // 2
            side = lax.rem(column + blocks * 2 * LANES, 2)
            block = lax.rem(at // LANES, blocks)
            after = lax.rem(at // LANES + 1, blocks)
            sources.append((side * blocks + block, side * blocks + after, at % LANES))

        def tile(t):
            return slice(SUB + t * SUB, 2 * SUB + t * SUB)

        def window(t, j):
            rows = pl.ds(start_row + t * SUB, SUB)
            out = []
            for block, after, shift in sources:
                back = lax.rem(LANES - shift, LANES)
                here = pltpu.roll(whole[block * slices + j, rows, :], back, 1)
                there = pltpu.roll(whole[after * slices + j, rows, :], back, 1)
                out.append(jnp.where(lane < LANES - shift, here, there))
            return out

        def phase(t, j):
            out = []
            for value in window(t, j):
                theta = value - 1.0
                z = theta * theta
                c = COS[4]
                s = SIN[4]
                for k in (3, 2, 1, 0):
                    c = c * z + COS[k]
                    s = s * z + SIN[k]
                out.append((c, s * theta))
            return out

        def laplace(ref, part, t):
            even, odd = (ref[part, p, tile(t)] for p in range(2))
            row = SUB + t * SUB
            even_rows = ref[part, 0, row - 1:row + SUB - 1] + ref[part, 0, row + 1:row + SUB + 1]
            odd_rows = ref[part, 1, row - 1:row + SUB - 1] + ref[part, 1, row + 1:row + SUB + 1]
            even_columns = odd + jnp.where(lane == 0, 0.0, pltpu.roll(odd, 1, 1))
            odd_columns = even + jnp.where(lane == LANES - 1, 0.0, pltpu.roll(even, LANES - 1, 1))
            return (even_rows + even_columns) - 4.0 * even, (odd_rows + odd_columns) - 4.0 * odd

        def step(src, dst, factor):
            for t in range(groups):
                lap_re = laplace(src, 0, t)
                lap_im = laplace(src, 1, t)
                for p in range(2):
                    dst[0, p, tile(t)] = base[0, p, tile(t)] - factor * lap_im[p]
                    dst[1, p, tile(t)] = base[1, p, tile(t)] + factor * lap_re[p]

        def propagate():
            step(base, ping, A_PROP / 4)
            step(ping, pong, A_PROP / 3)
            step(pong, ping, A_PROP / 2)
            step(ping, pong, A_PROP)

        def enter(t, j, source, offset, kept):
            for p, (c, s) in enumerate(phase(t, j)):
                re = source[0, p, pl.ds(offset + t * SUB, SUB)]
                im = source[1, p, pl.ds(offset + t * SUB, SUB)]
                new_re, new_im = re * c - im * s, re * s + im * c
                base[0, p, tile(t)] = new_re
                base[1, p, tile(t)] = new_im
                kept[0, p, tile(t)] = new_re
                kept[1, p, tile(t)] = new_im
                if j == slices - 1:
                    turn[0, p, tile(t)] = c
                    turn[1, p, tile(t)] = s

        def leave(t, j, kept):
            rows = pl.ds(start_row + t * SUB, SUB)
            for p, (block, after, shift) in enumerate(sources):
                re = pong[0, p, tile(t)]
                im = pong[1, p, tile(t)]
                grad = -(re * kept[1, p, tile(t)] + im * kept[0, p, tile(t)])
                if j:
                    c = turn[0, p, tile(t)]
                    s = turn[1, p, tile(t)]
                    base[0, p, tile(t)] = re * c - im * s
                    base[1, p, tile(t)] = re * s + im * c
                rolled = pltpu.roll(grad, shift, 1)
                here = block * slices + j
                there = after * slices + j
                total[here, rows, :] = total[here, rows, :] + jnp.where(lane < shift, 0.0, rolled)
                total[there, rows, :] = total[there, rows, :] + jnp.where(lane < shift, rolled, 0.0)

        def dot(a, b):
            return jnp.dot(a[...], b[...], preferred_element_type=jnp.float32)

        def put_stack(stack, part, p, value):
            high, low = split(value)
            for k, piece in enumerate((high, low, high)):
                stack[k * size + part * half:k * size + (part + 1) * half, p * LANES:(p + 1) * LANES] = piece

        def put_wide(wide, rows, part, value):
            high, low = split(value)
            for k, piece in enumerate((high, low, high)):
                wide[rows, k * size + part * half:k * size + (part + 1) * half] = piece

        def lanes(k):
            return slice(k * LANES, (k + 1) * LANES)

        for t in range(groups):
            enter(t, 0, probe_ref, 0, first)
        propagate()
        for t in range(groups):
            enter(t, 1, pong, SUB, second)
        propagate()

        upper, lower = slice(0, half), slice(half, size)
        for part in range(2):
            for p in range(2):
                top = pong[part, p, SUB:SUB + half]
                bottom = pong[part, p, SUB + half:SUB + size]
                put_stack(stack_even, part, p, top + bottom)
                put_stack(stack_odd, part, p, top - bottom)
        for rows, inner in ((upper, dot(left_even, stack_even)), (lower, dot(left_odd, stack_odd))):
            for part, own in enumerate((upper, lower)):
                put_wide(wide_even, rows, part, inner[own, lanes(0)])
                put_wide(wide_odd, rows, part, inner[own, lanes(1)])
        even = dot(wide_even, right_even)
        odd = dot(wide_odd, right_odd)
        for k, rows in enumerate((upper, lower)):
            pulled = []
            for sign, data in ((1, low_ref), (-1, high_ref)):
                far_re = even[rows, lanes(0)] + sign * odd[rows, lanes(0)]
                far_im = even[rows, lanes(1)] + sign * odd[rows, lanes(1)]
                excess = (far_re * far_re + far_im * far_im) - data[pl.ds(k, half, stride=2), :]
                scaled = (4.0 * LOSS_SCALE) * excess
                pulled.append((scaled * far_re, -(scaled * far_im)))
            for part in range(2):
                put_wide(wide_even, rows, part, pulled[0][part] + pulled[1][part])
                put_wide(wide_odd, rows, part, pulled[0][part] - pulled[1][part])
        for p, inner in enumerate((dot(wide_even, right_even), dot(wide_odd, right_odd_back))):
            for part in range(2):
                put_stack(stack_even, part, p, inner[upper, lanes(part)])
                put_stack(stack_odd, part, p, inner[lower, lanes(part)])
        even = dot(left_even, stack_even)
        odd = dot(left_odd_back, stack_odd)
        for part, own in enumerate((upper, lower)):
            for p in range(2):
                base[part, p, SUB:SUB + half] = even[own, lanes(p)] + odd[own, lanes(p)]
                base[part, p, SUB + half:SUB + size] = even[own, lanes(p)] - odd[own, lanes(p)]

        propagate()
        for t in range(groups):
            leave(t, 1, second)
        propagate()
        for t in range(groups):
            leave(t, 0, first)

    @pl.when(slot == pl.num_programs(0) - 1)
    def _():
        copies = [
            pltpu.make_async_copy(total.at[:, rows_of(offset, 1), :], outs[offset[0] * grid[2] + offset[2]].at[offset[1]], sems.at[0])
            for offset in offsets
        ]
        for copy in copies:
            copy.start()
        for copy in copies:
            copy.wait()


def window_gradients(rows, columns, count, place, pieces, grid, probe, measured, slices, zero):
    slots, size = measured.shape[:2]
    planes, height, _ = pieces[0].shape
    peers = len(pieces)
    blocks = planes // (2 * slices)
    factors = tables(size, zero)
    full = lambda a: pl.BlockSpec(a.shape, lambda k, *_: (0,) * a.ndim)
    anywhere = pl.BlockSpec(memory_space=pl.ANY)
    field = pltpu.VMEM((2, 2, size + 2 * SUB, LANES), jnp.float32)
    plane = pltpu.VMEM((planes, peers * height, LANES), jnp.float32)
    tall = pltpu.VMEM((3 * size, size), jnp.bfloat16)
    wide = pltpu.VMEM((size, 3 * size), jnp.bfloat16)
    groups = grid[0] * grid[2]

    def body(*refs):
        scalars, refs = refs[:4], refs[4:]
        fixed, refs = refs[:9], refs[9:]
        return kernel(
            *scalars, *fixed, refs[:peers], refs[peers:peers + groups], *refs[peers + groups:],
            blocks=blocks, slices=slices, grid=grid,
        )

    return pl.pallas_call(
        body,
        grid_spec=pltpu.PrefetchScalarGridSpec(
            num_scalar_prefetch=4,
            grid=(slots,),
            in_specs=[
                full(probe),
                pl.BlockSpec((None, size, LANES), lambda k, *_: (k, 0, 0)),
                pl.BlockSpec((None, size, LANES), lambda k, *_: (k, 0, 1)),
                *[full(f) for f in factors],
                *[anywhere for _ in pieces],
            ],
            out_specs=[anywhere] * groups,
            scratch_shapes=[plane, plane] + [field] * 6 + [tall, tall, wide, wide, pltpu.SemaphoreType.DMA((1,))],
        ),
        out_shape=[jax.ShapeDtypeStruct((grid[1], planes, height, LANES), jnp.float32)] * groups,
        compiler_params=pltpu.CompilerParams(vmem_limit_bytes=48 * 2**20),
        name="windows",
    )(rows, columns, count, place, probe, measured, measured, *factors, *pieces)


def grid_of(devices):
    count = len(devices)
    cores = len({d.core_on_chip for d in devices})
    chips = [tuple(devices[i].coords) for i in range(0, count, cores)]
    fast = 1
    if len(chips) > 1:
        moving = [a != b for a, b in zip(chips[0], chips[1])]
        while fast < len(chips) and all(m or a == b for m, a, b in zip(moving, chips[0], chips[fast])):
            fast += 1
    if len(chips) % fast:
        fast = 1
    return len(chips) // fast, fast, cores


def shards(potential, probe_wave, offsets, members, counts, measured, *, grid):
    slices, height, own_width = potential.shape
    size = probe_wave.shape[-1]
    strips = lax.axis_size("strip")
    up = [(i, i + 1) for i in range(strips - 1)]
    down = [(j, i) for i, j in up]
    slow, fast, cores = grid

    def moved(value, a, b, c):
        if not (a or b or c):
            return value
        pairs = []
        for z in range(slow):
            for y in range(fast):
                for core in range(cores):
                    to = ((z + a) % slow * fast + (y + b) % fast) * cores + (core + c) % cores
                    pairs.append(((z * fast + y) * cores + core, to))
        return lax.ppermute(value, "probe", pairs)

    def along(value, to, valid):
        pairs = []
        for z in range(slow):
            if 0 <= z + to < slow and valid(z + to):
                for rest in range(fast * cores):
                    pairs.append((z * fast * cores + rest, (z + to) * fast * cores + rest))
        return lax.ppermute(value, "probe", pairs)

    def after(value, *done):
        return lax.optimization_barrier((value, *done))[0]

    flat = potential.reshape(slices * height, own_width)
    from_left = lax.ppermute(flat[:, own_width - EDGE:], "strip", up)
    from_right = lax.ppermute(flat[:, :EDGE], "strip", down)
    piece = deal(flat, from_right, from_left)
    piece, probe_wave, offsets, members, zero = lax.optimization_barrier(
        (piece, probe_wave, offsets, members, jnp.zeros((), jnp.int32))
    )
    blocks = piece.shape[1]
    piece = piece.reshape(2 * blocks * slices, height, LANES)

    lines = {0: piece}
    if slow > 1:
        lines[1] = moved(piece, 1, 0, 0)
    if slow > 2:
        lines[slow - 1] = moved(after(piece, lines[1]), slow - 1, 0, 0)
        right, left = {1: lines[1]}, {1: lines[slow - 1]}
        for k in range(2, slow - 1):
            right[k] = along(right[k - 1], 1, lambda z: z >= k)
            left[k] = along(left[k - 1], -1, lambda z: z <= slow - 1 - k)
        for k in range(2, slow - 1):
            lines[k] = right[k] + left[slow - k]
    order = [0] + [k for k in (1, slow - 1) if 0 < k < slow] + list(range(2, slow - 1))
    order = list(dict.fromkeys(order))
    held = {}
    previous = None
    for a in order:
        held[a, 0] = lines[a]
        for b in range(1, fast):
            source = lines[a] if previous is None else after(lines[a], previous)
            previous = held[a, b] = moved(source, 0, b, 0)
    pieces = []
    for a in range(slow):
        for b in range(fast):
            for c in range(cores):
                pieces.append(moved(held[a, b], 0, 0, c))

    positions = members[0, 0]
    rows = offsets[0, 0][positions]
    columns = offsets[0, 1][positions]
    me = lax.axis_index("probe")
    place = jnp.stack([me // (fast * cores), me // cores % fast, me % cores]).astype(jnp.int32)
    probe = deal(probe_wave.reshape(2 * size, size)).reshape(2, 2, size, LANES).transpose(1, 0, 2, 3)
    terms = window_gradients(rows, columns, counts[0], place, pieces, grid, probe, measured[0, 0], slices, zero)

    chip = {}
    for a in range(slow):
        own = terms[a * cores]
        for c in range(1, cores):
            own = own + moved(terms[a * cores + c], 0, 0, c)
        chip[a] = own
    line = {}
    previous = None
    for a in reversed(order):
        total = chip[a][0]
        for b in range(1, fast):
            source = chip[a][b] if previous is None else after(chip[a][b], previous)
            previous = moved(source, 0, b, 0)
            total = total + previous
        line[a] = total
    mine = [line[0]]
    right, left = None, None
    for k in range(slow - 2, 1, -1):
        right = line[k] if right is None else line[k] + right
        left = line[slow - k] if left is None else line[slow - k] + left
        right = along(right, 1, lambda z: z <= slow - k)
        left = along(left, -1, lambda z: z >= k - 1)
    if slow > 1:
        first = line[1] if right is None else line[1] + right
        mine.append(moved(first, 1, 0, 0))
    if slow > 2:
        last = line[slow - 1] if left is None else line[slow - 1] + left
        mine.append(moved(last, slow - 1, 0, 0))
    mine = [term.reshape(2, blocks, slices * height, LANES) for term in mine]
    edges = sum(term[:, -1] for term in mine[1:]) + mine[0][:, -1]
    from_left = lax.ppermute(edges, "strip", up)
    from_right = lax.ppermute(edges, "strip", down)
    return weave(mine, from_left, from_right).reshape(potential.shape)


def solution(mesh):
    placed = (
        P(None, "probe", "strip"),
        P(),
        P("strip", None, None),
        P("strip", "probe", None),
        P("strip", "probe"),
        P("strip", "probe", None, None, None),
    )
    grid = grid_of(list(mesh.devices[:, 0]))
    return jax.shard_map(
        functools.partial(shards, grid=grid), mesh=mesh, in_specs=placed, out_specs=P(None, "probe", "strip"), check_vma=False
    )
```

```python
import functools
import math

import jax
import jax.numpy as jnp
from jax import lax
from jax.experimental import pallas as pl
from jax.experimental.pallas import tpu as pltpu
from jax.sharding import PartitionSpec as P

EDGE = 128
A_PROP = 0.1
LOSS_SCALE = 0.03125
LANES = 128
SUB = 8
COS = (0.9999999993567104, -0.4999999690796125, 0.041666428711172335, -0.0013882473076505886, 2.4093931432702378e-05)
SIN = (0.9999999999413409, -0.1666666638472293, 0.008333311638477454, -0.00019835422091007726, 2.6912728384156356e-06)


def split(value):
    high = value.astype(jnp.bfloat16)
    return high, (value - high.astype(jnp.float32)).astype(jnp.bfloat16)


def split_table(value):
    high = lax.reduce_precision(value, 8, 7)
    return high.astype(jnp.bfloat16), (value - high).astype(jnp.bfloat16)


def tables(size, zero):
    half = jnp.arange(size // 2, dtype=jnp.int32) + zero

    def wave(exponents):
        angles = -2.0 * math.pi / size * (exponents % size).astype(jnp.float32)
        scale = 1.0 / math.sqrt(size)
        return jnp.cos(angles) * scale, jnp.sin(angles) * scale

    def left(real, imag):
        high, low = split_table(jnp.block([[real, -imag], [imag, real]]))
        return jnp.concatenate([high, high, low], 1)

    def right(real, imag):
        high, low = split_table(jnp.block([[real, imag], [-imag, real]]))
        return jnp.concatenate([high, high, low], 0)

    even = wave(2 * half[:, None] * half[None, :])
    odd = wave((2 * half[:, None] + 1) * half[None, :])
    odd_back = wave(half[:, None] * (2 * half[None, :] + 1))
    return left(*even), left(*odd), left(*odd_back), right(*even), right(*odd), right(*odd_back)


def parity(width):
    columns = lax.broadcasted_iota(jnp.int32, (width, width), 1)
    rows = lax.broadcasted_iota(jnp.int32, (width, width), 0)
    source = columns % (width // 2) * 2 + columns // (width // 2)
    return (rows == source).astype(jnp.float32).astype(jnp.bfloat16)


def exact_dot(value, selection):
    high = value.astype(jnp.bfloat16)
    rest = value - high.astype(jnp.float32)
    middle = rest.astype(jnp.bfloat16)
    low = (rest - middle.astype(jnp.float32)).astype(jnp.bfloat16)
    total = jnp.dot(high, selection, preferred_element_type=jnp.float32)
    total = total + jnp.dot(middle, selection, preferred_element_type=jnp.float32)
    return total + jnp.dot(low, selection, preferred_element_type=jnp.float32)


def deal_kernel(flags_ref, x_ref, *refs):
    *edges, o_ref = refs
    pair = 2 * LANES
    selection = parity(pair)
    for block in range(o_ref.shape[2]):
        if block * pair < x_ref.shape[1]:
            value = x_ref[:, block * pair:(block + 1) * pair]
        else:
            value = jnp.concatenate(
                [jnp.where(flags_ref[k] > 0, ref[...], 0.0) for k, ref in zip((1, 0), edges)], 1
            )
        dealt = exact_dot(value, selection)
        height = o_ref.shape[3]
        for j in range(o_ref.shape[0]):
            for p in range(2):
                o_ref[j, p, block] = dealt[j * height:(j + 1) * height, p * LANES:(p + 1) * LANES]


def deal(flags, value, slices, *edges):
    rows, width = value.shape
    blocks = (width + sum(e.shape[1] for e in edges)) // (2 * LANES)
    vmem = pl.BlockSpec(memory_space=pltpu.VMEM)
    return pl.pallas_call(
        deal_kernel,
        in_specs=[pl.BlockSpec(memory_space=pltpu.SMEM)] + [vmem] * (1 + len(edges)),
        out_specs=vmem,
        out_shape=jax.ShapeDtypeStruct((slices, 2, blocks, rows // slices, LANES), jnp.float32),
        name="deal",
    )(flags, value, *edges)


def weave_kernel(flags_ref, *refs):
    *terms, left_ref, right_ref, o_ref = refs
    pair = 2 * LANES
    rows = lax.broadcasted_iota(jnp.int32, (pair, pair), 0)
    columns = lax.broadcasted_iota(jnp.int32, (pair, pair), 1)
    selection = (columns == rows % LANES * 2 + rows // LANES).astype(jnp.float32).astype(jnp.bfloat16)
    lane = lax.broadcasted_iota(jnp.int32, terms[0].shape[3:], 1)
    blocks = o_ref.shape[1] // pair
    for k in range(blocks):
        parts = []
        for p in range(2):
            stacked = []
            for j in range(terms[0].shape[0]):
                value = terms[0][j, p, k]
                for term in terms[1:]:
                    value = value + term[j, p, k]
                if k == 0:
                    value = value + jnp.where((lane < EDGE // 2) & (flags_ref[0] > 0), left_ref[j, p], 0.0)
                if k == blocks - 1:
                    value = value + jnp.where((lane >= LANES - EDGE // 2) & (flags_ref[1] > 0), right_ref[j, p], 0.0)
                stacked.append(value)
            parts.append(jnp.concatenate(stacked, 0))
        o_ref[:, k * pair:(k + 1) * pair] = exact_dot(jnp.concatenate(parts, 1), selection)


def weave(flags, terms, from_left, from_right):
    slices, _, blocks, height, _ = terms[0].shape
    vmem = pl.BlockSpec(memory_space=pltpu.VMEM)
    return pl.pallas_call(
        weave_kernel,
        in_specs=[pl.BlockSpec(memory_space=pltpu.SMEM)] + [vmem] * (2 + len(terms)),
        out_specs=vmem,
        out_shape=jax.ShapeDtypeStruct((slices * height, (blocks - 1) * 2 * LANES), jnp.float32),
        name="weave",
    )(flags, *terms, from_left, from_right)


def kernel(
    rows_ref, columns_ref, count_ref,
    sources_ref, targets_ref, low_ref, high_ref,
    fixed, pieces, outs,
    whole, total, base, ping, pong, first, second, turn, stack_even, stack_odd, wide_even, wide_odd,
    probe_ref, left_even, left_odd, left_odd_back, right_even, right_odd, right_odd_back, sems,
    *, blocks, slices, spans, out_spans,
):
    slot = pl.program_id(0)
    size = low_ref.shape[0]
    half = size // 2
    groups = size // SUB
    height = pieces[0].shape[1]

    lane = lax.broadcasted_iota(jnp.int32, (SUB, LANES), 1)

    layer = 2 * blocks

    def layers(refs_and_rows, span, j):
        piece, ref, start = refs_and_rows
        low, high = j * layer, (j + 1) * layer
        if span.start > low or span.stop < high:
            return []
        rows = pl.ds(pl.multiple_of(start, height), height)
        return [(piece.at[low - span.start:high - span.start], ref.at[low:high, rows, :])]

    def loads(j):
        out = []
        for k, (piece, span) in enumerate(zip(pieces, spans)):
            for source, target in layers((piece, whole, sources_ref[k]), span, j):
                out.append(pltpu.make_async_copy(source, target, sems.at[j]))
        if j == 0:
            out.append(pltpu.make_async_copy(fixed[0], probe_ref, sems.at[j]))
        else:
            factors = (left_even, left_odd, left_odd_back, right_even, right_odd, right_odd_back)
            out += [pltpu.make_async_copy(a, b, sems.at[j]) for a, b in zip(fixed[1:], factors)]
        return out

    def stores(j):
        out = []
        for piece, (index, span) in zip(outs, out_spans):
            for target, source in layers((piece, total, targets_ref[index]), span, j):
                out.append(pltpu.make_async_copy(source, target, sems.at[slices + j]))
        return out

    last = slot == pl.num_programs(0) - 1

    @pl.when(slot == 0)
    def _():
        for j in range(slices):
            for copy in loads(j):
                copy.start()

        def clear(i, carry):
            for k in range(total.shape[0]):
                total[k, pl.ds(pl.multiple_of(i * SUB, SUB), SUB), :] = jnp.zeros((SUB, LANES), jnp.float32)
            return carry
        lax.fori_loop(0, total.shape[1] // SUB, clear, 0)
        for field in (base, ping, pong):
            for part in range(2):
                for p in range(2):
                    field[part, p, :SUB] = jnp.zeros((SUB, LANES), jnp.float32)
                    field[part, p, SUB + size:] = jnp.zeros((SUB, LANES), jnp.float32)
        for copy in loads(0):
            copy.wait()

    def compute(stage):
        start_row = rows_ref[slot]
        start_column = columns_ref[slot]
        sources = []
        for p in range(2):
            column = start_column + p
            at = (column + blocks * 2 * LANES) // 2
            side = lax.rem(column + blocks * 2 * LANES, 2)
            block = lax.rem(at // LANES, blocks)
            after = lax.rem(at // LANES + 1, blocks)
            sources.append((side * blocks + block, side * blocks + after, at % LANES))

        def tile(t):
            return slice(SUB + t * SUB, 2 * SUB + t * SUB)

        def window(t, j):
            rows = pl.ds(start_row + t * SUB, SUB)
            out = []
            for block, after, shift in sources:
                back = lax.rem(LANES - shift, LANES)
                here = pltpu.roll(whole[j * layer + block, rows, :], back, 1)
                there = pltpu.roll(whole[j * layer + after, rows, :], back, 1)
                out.append(jnp.where(lane < LANES - shift, here, there))
            return out

        def phase(t, j):
            out = []
            for value in window(t, j):
                theta = value - 1.0
                z = theta * theta
                c = COS[4]
                s = SIN[4]
                for k in (3, 2, 1, 0):
                    c = c * z + COS[k]
                    s = s * z + SIN[k]
                out.append((c, s * theta))
            return out

        def laplace(ref, part, t):
            even, odd = (ref[part, p, tile(t)] for p in range(2))
            row = SUB + t * SUB
            even_rows = ref[part, 0, row - 1:row + SUB - 1] + ref[part, 0, row + 1:row + SUB + 1]
            odd_rows = ref[part, 1, row - 1:row + SUB - 1] + ref[part, 1, row + 1:row + SUB + 1]
            even_columns = odd + jnp.where(lane == 0, 0.0, pltpu.roll(odd, 1, 1))
            odd_columns = even + jnp.where(lane == LANES - 1, 0.0, pltpu.roll(even, LANES - 1, 1))
            return (even_rows + even_columns) - 4.0 * even, (odd_rows + odd_columns) - 4.0 * odd

        def step(src, dst, factor):
            for t in range(groups):
                lap_re = laplace(src, 0, t)
                lap_im = laplace(src, 1, t)
                for p in range(2):
                    dst[0, p, tile(t)] = base[0, p, tile(t)] - factor * lap_im[p]
                    dst[1, p, tile(t)] = base[1, p, tile(t)] + factor * lap_re[p]

        def propagate():
            step(base, ping, A_PROP / 4)
            step(ping, pong, A_PROP / 3)
            step(pong, ping, A_PROP / 2)
            step(ping, pong, A_PROP)

        def enter(t, j, source, offset, kept):
            for p, (c, s) in enumerate(phase(t, j)):
                re = source[0, p, pl.ds(offset + t * SUB, SUB)]
                im = source[1, p, pl.ds(offset + t * SUB, SUB)]
                new_re, new_im = re * c - im * s, re * s + im * c
                base[0, p, tile(t)] = new_re
                base[1, p, tile(t)] = new_im
                kept[0, p, tile(t)] = new_re
                kept[1, p, tile(t)] = new_im
                if j == slices - 1:
                    turn[0, p, tile(t)] = c
                    turn[1, p, tile(t)] = s

        def leave(tiles, j, kept):
            sums = []
            for t in tiles:
                rows = pl.ds(start_row + t * SUB, SUB)
                for p, (block, after, shift) in enumerate(sources):
                    re = pong[0, p, tile(t)]
                    im = pong[1, p, tile(t)]
                    grad = -(re * kept[1, p, tile(t)] + im * kept[0, p, tile(t)])
                    if j:
                        c = turn[0, p, tile(t)]
                        s = turn[1, p, tile(t)]
                        base[0, p, tile(t)] = re * c - im * s
                        base[1, p, tile(t)] = re * s + im * c
                    rolled = pltpu.roll(grad, shift, 1)
                    here = j * layer + block
                    there = j * layer + after
                    sums.append((here, rows, total[here, rows, :] + jnp.where(lane < shift, 0.0, rolled)))
                    sums.append((there, rows, total[there, rows, :] + jnp.where(lane < shift, rolled, 0.0)))
            for plane, rows, value in sums:
                total[plane, rows, :] = value

        def dot(a, b):
            return jnp.dot(a[...], b[...], preferred_element_type=jnp.float32)

        def put_stack(stack, part, p, value):
            high, low = split(value)
            for k, piece in enumerate((high, low, high)):
                stack[k * size + part * half:k * size + (part + 1) * half, p * LANES:(p + 1) * LANES] = piece

        def put_wide(wide, rows, part, value):
            high, low = split(value)
            for k, piece in enumerate((high, low, high)):
                wide[rows, k * size + part * half:k * size + (part + 1) * half] = piece

        def lanes(k):
            return slice(k * LANES, (k + 1) * LANES)

        if stage == 0:
            for t in range(groups):
                enter(t, 0, probe_ref, 0, first)
            propagate()
            return
        if stage == 2:
            propagate()
            for t in range(0, groups, 8):
                leave(range(t, t + 8), 0, first)
            return
        for t in range(groups):
            enter(t, 1, pong, SUB, second)
        propagate()

        upper, lower = slice(0, half), slice(half, size)
        for part in range(2):
            for p in range(2):
                top = pong[part, p, SUB:SUB + half]
                bottom = pong[part, p, SUB + half:SUB + size]
                put_stack(stack_even, part, p, top + bottom)
                put_stack(stack_odd, part, p, top - bottom)
        for rows, inner in ((upper, dot(left_even, stack_even)), (lower, dot(left_odd, stack_odd))):
            for part, own in enumerate((upper, lower)):
                put_wide(wide_even, rows, part, inner[own, lanes(0)])
                put_wide(wide_odd, rows, part, inner[own, lanes(1)])
        even = dot(wide_even, right_even)
        odd = dot(wide_odd, right_odd)
        for k, rows in enumerate((upper, lower)):
            pulled = []
            for sign, data in ((1, low_ref), (-1, high_ref)):
                far_re = even[rows, lanes(0)] + sign * odd[rows, lanes(0)]
                far_im = even[rows, lanes(1)] + sign * odd[rows, lanes(1)]
                excess = (far_re * far_re + far_im * far_im) - data[pl.ds(k, half, stride=2), :]
                scaled = (4.0 * LOSS_SCALE) * excess
                pulled.append((scaled * far_re, -(scaled * far_im)))
            for part in range(2):
                put_wide(wide_even, rows, part, pulled[0][part] + pulled[1][part])
                put_wide(wide_odd, rows, part, pulled[0][part] - pulled[1][part])
        for p, inner in enumerate((dot(wide_even, right_even), dot(wide_odd, right_odd_back))):
            for part in range(2):
                put_stack(stack_even, part, p, inner[upper, lanes(part)])
                put_stack(stack_odd, part, p, inner[lower, lanes(part)])
        even = dot(left_even, stack_even)
        odd = dot(left_odd_back, stack_odd)
        for part, own in enumerate((upper, lower)):
            for p in range(2):
                base[part, p, SUB:SUB + half] = even[own, lanes(p)] + odd[own, lanes(p)]
                base[part, p, SUB + half:SUB + size] = even[own, lanes(p)] - odd[own, lanes(p)]

        propagate()
        for t in range(0, groups, 8):
            leave(range(t, t + 8), 1, second)

    used = slot < count_ref[0]
    pl.when(used)(lambda: compute(0))

    @pl.when(slot == 0)
    def _():
        for j in range(1, slices):
            for copy in loads(j):
                copy.wait()

    pl.when(used)(lambda: compute(1))

    @pl.when(last)
    def _():
        for j in range(1, slices):
            for copy in stores(j):
                copy.start()

    pl.when(used)(lambda: compute(2))

    @pl.when(last)
    def _():
        for copy in stores(0):
            copy.start()
        for j in range(slices):
            for copy in stores(j):
                copy.wait()


def window_gradients(rows, columns, count, sources, targets, pieces, spans, out_spans, probe, measured, slices, planes, factors):
    slots, size = measured.shape[:2]
    height = pieces[0].shape[1]
    blocks = planes // (2 * slices)
    anywhere = pl.BlockSpec(memory_space=pl.ANY)
    field = pltpu.VMEM((2, 2, size + 2 * SUB, LANES), jnp.float32)
    plane = pltpu.VMEM((planes, targets.shape[0] * height, LANES), jnp.float32)
    tall = pltpu.VMEM((3 * size, size), jnp.bfloat16)
    wide = pltpu.VMEM((size, 3 * size), jnp.bfloat16)
    count_in, count_out = len(pieces), len(out_spans)

    fixed = (probe, *factors)

    def body(*refs):
        head, held, refs = refs[:7], refs[7:7 + len(fixed)], refs[7 + len(fixed):]
        return kernel(
            *head, held, refs[:count_in], refs[count_in:count_in + count_out], *refs[count_in + count_out:],
            blocks=blocks, slices=slices, spans=spans, out_spans=out_spans,
        )

    return pl.pallas_call(
        body,
        grid_spec=pltpu.PrefetchScalarGridSpec(
            num_scalar_prefetch=5,
            grid=(slots,),
            in_specs=[
                pl.BlockSpec((None, size, LANES), lambda k, *_: (k, 0, 0)),
                pl.BlockSpec((None, size, LANES), lambda k, *_: (k, 0, 1)),
                *[anywhere for _ in (*fixed, *pieces)],
            ],
            out_specs=[anywhere] * count_out,
            scratch_shapes=[plane, plane] + [field] * 6 + [tall, tall, wide, wide]
            + [pltpu.VMEM(f.shape, f.dtype) for f in fixed] + [pltpu.SemaphoreType.DMA((2 * slices,))],
        ),
        out_shape=[
            jax.ShapeDtypeStruct((span.stop - span.start, height, LANES), jnp.float32) for _, span in out_spans
        ],
        compiler_params=pltpu.CompilerParams(vmem_limit_bytes=48 * 2**20),
        name="windows",
    )(rows, columns, count, sources, targets, measured, measured, *fixed, *pieces)


def ring_of(slow, fast):
    if slow % 2 and fast % 2 == 0:
        return [y * fast + x for x, y in ((c // slow, c % slow) for c in ring_of(fast, slow))]
    if fast == 1 or slow % 2:
        return list(range(slow * fast))
    path = []
    for z in range(slow):
        row = range(1, fast)
        path += [z * fast + y for y in (row if z % 2 == 0 else reversed(row))]
    return path + [z * fast for z in reversed(range(slow))]


def grid_of(devices):
    count = len(devices)
    cores = len({d.core_on_chip for d in devices})
    chips = [tuple(devices[i].coords) for i in range(0, count, cores)]
    fast = 1
    if len(chips) > 1:
        moving = [a != b for a, b in zip(chips[0], chips[1])]
        while fast < len(chips) and all(m or a == b for m, a, b in zip(moving, chips[0], chips[fast])):
            fast += 1
    if len(chips) % fast:
        fast = 1
    return len(chips) // fast, fast, cores


def shards(potential, probe_wave, offsets, members, counts, measured, *, grid):
    slices, height, own_width = potential.shape
    size = probe_wave.shape[-1]
    strips = lax.axis_size("strip")
    strip = lax.axis_index("strip")
    flags = jnp.stack([strip > 0, strip < strips - 1]).astype(jnp.int32)
    slow, fast, cores = grid
    ring = ring_of(slow, fast)
    chips = len(ring)
    reach = (chips - 1) // 2

    def to_neighbours(rightward, leftward):
        if strips == 2:
            sent = rightward if rightward is leftward else jnp.where(strip == 0, rightward, leftward)
            got = lax.ppermute(sent, "strip", [(0, 1), (1, 0)])
            return got, got
        ahead = [(i, (i + 1) % strips) for i in range(strips)]
        return lax.ppermute(rightward, "strip", ahead), lax.ppermute(leftward, "strip", [(j, i) for i, j in ahead])

    def around(value, by):
        pairs = []
        for k, chip in enumerate(ring):
            for core in range(cores):
                pairs.append((chip * cores + core, ring[(k + by) % chips] * cores + core))
        return lax.ppermute(value, "probe", pairs)

    def inside(value, by):
        if by == 0:
            return value
        pairs = [(chip * cores + c, chip * cores + (c + by) % cores) for chip in range(chips) for c in range(cores)]
        return lax.ppermute(value, "probe", pairs)

    flat = potential.reshape(slices * height, own_width)
    from_left, from_right = to_neighbours(flat[:, own_width - EDGE:], flat[:, :EDGE])
    piece = deal(flags, flat, slices, from_right, from_left)
    piece, probe_wave, offsets, members, zero = lax.optimization_barrier(
        (piece, probe_wave, offsets, members, jnp.zeros((), jnp.int32))
    )
    blocks = piece.shape[2]
    planes = 2 * blocks * slices
    every, upper, lower = slice(0, planes), slice(0, planes // 2), slice(planes // 2, planes)
    piece = piece.reshape(planes, height, LANES)

    order = jnp.array(ring, jnp.int32)
    far = [(chips // 2, upper), (chips // 2, lower)] if chips % 2 == 0 else []
    near = [(s * d, every) for d in range(1, reach + 1) for s in (-1, 1)]
    offsets_in, spans = [], []
    for d, span in [(0, every), *near, *far]:
        for c in range(cores):
            spans.append(span)
            offsets_in.append((d, -c))
    out_spans, offsets_out = [], []
    for d in range(-reach, chips - reach):
        for c in range(cores):
            halves = (upper, lower) if 2 * d == chips else (every,)
            out_spans += [(len(offsets_out), span) for span in halves]
            offsets_out.append((d, c))

    def fields(zero):
        positions = members[0, 0] + zero
        probe = deal(flags, probe_wave.reshape(2 * size, size), 2).reshape(2, 2, size, LANES)
        return offsets[0, 0][positions], offsets[0, 1][positions], probe

    def places(zero):
        me = lax.axis_index("probe") + zero
        seat = jnp.sum(jnp.where(order == me // cores, jnp.arange(chips, dtype=jnp.int32), 0))
        out = []
        for listed in (offsets_in, offsets_out):
            d, c = (jnp.array(v, jnp.int32) for v in zip(*listed))
            chip = jnp.sum(jnp.where(((seat + d + chips) % chips)[:, None] == jnp.arange(chips), order, 0), 1)
            out.append((chip * cores + (me % cores + c + cores) % cores) * height)
        return out

    chores = [fields, lambda zero: tables(size, zero), places]
    done = []

    def beside(zero, *moving):
        if chores and len(done) < len(chores):
            *moving, zero, made = lax.optimization_barrier((*moving, zero, tuple(chores[len(done)](zero))))
            done.append(made)
        return (zero, *moving)

    waiting, pieces = [piece], []

    def share(value):
        pieces.extend(inside(value, c) for c in range(cores))

    ahead = behind = piece
    for d in range(1, reach + 1):
        ahead = around(ahead, 1)
        behind = around(behind, -1)
        zero, ahead, behind = beside(zero, ahead, behind)
        for value in waiting:
            share(lax.optimization_barrier((value, ahead, behind))[0])
        waiting = [ahead, behind]
    if chips % 2 == 0:
        waiting += [around(ahead[upper], 1), around(behind[lower], -1)]
    for value in waiting:
        share(value)
    while len(done) < len(chores):
        beside(zero)
    (rows, columns, probe), factors, (sources, targets) = done
    terms = window_gradients(
        rows, columns, counts[0], sources, targets, pieces, spans, out_spans, probe,
        measured[0, 0], slices, planes, factors,
    )

    by_place = {}
    for (index, span), term in zip(out_spans, terms):
        by_place.setdefault((*offsets_out[index], span.start), term)

    def on_chip(d, start=0):
        own = by_place[d, 0, start]
        for c in range(1, cores):
            own = own + inside(by_place[d, c, start], c)
        return own

    ahead = behind = None
    if chips % 2 == 0:
        ahead = jnp.pad(around(on_chip(chips // 2), 1), ((0, planes // 2), (0, 0), (0, 0)))
        behind = jnp.pad(around(on_chip(chips // 2, planes // 2), -1), ((planes // 2, 0), (0, 0), (0, 0)))
    for d in range(reach, 0, -1):
        ahead = around(on_chip(d) if ahead is None else on_chip(d) + ahead, 1)
        behind = around(on_chip(-d) if behind is None else on_chip(-d) + behind, -1)
    mine = [v.reshape(slices, 2, blocks, height, LANES) for v in (on_chip(0), ahead, behind) if v is not None]
    edges = sum(term[:, :, -1] for term in mine[1:]) + mine[0][:, :, -1]
    return weave(flags, mine, *to_neighbours(edges, edges)).reshape(potential.shape)


def solution(mesh):
    placed = (
        P(None, "probe", "strip"),
        P(),
        P("strip", None, None),
        P("strip", "probe", None),
        P("strip", "probe"),
        P("strip", "probe", None, None, None),
    )
    grid = grid_of(list(mesh.devices[:, 0]))
    return jax.shard_map(
        functools.partial(shards, grid=grid), mesh=mesh, in_specs=placed, out_specs=P(None, "probe", "strip"), check_vma=False
    )
```

```python
import functools
import math

import jax
import jax.numpy as jnp
from jax import lax
from jax.experimental import pallas as pl
from jax.experimental.pallas import tpu as pltpu
from jax.sharding import PartitionSpec as P

EDGE = 128
A_PROP = 0.1
LOSS_SCALE = 0.03125
LANES = 128
SUB = 8
COS = (0.9999999993567104, -0.4999999690796125, 0.041666428711172335, -0.0013882473076505886, 2.4093931432702378e-05)
SIN = (0.9999999999413409, -0.1666666638472293, 0.008333311638477454, -0.00019835422091007726, 2.6912728384156356e-06)


def split(value):
    high = value.astype(jnp.bfloat16)
    return high, (value - high.astype(jnp.float32)).astype(jnp.bfloat16)


def split_table(value):
    high = lax.reduce_precision(value, 8, 7)
    return high.astype(jnp.bfloat16), (value - high).astype(jnp.bfloat16)


def tables(size, zero):
    half = jnp.arange(size // 2, dtype=jnp.int32) + zero

    def wave(exponents):
        angles = -2.0 * math.pi / size * (exponents % size).astype(jnp.float32)
        scale = 1.0 / math.sqrt(size)
        return jnp.cos(angles) * scale, jnp.sin(angles) * scale

    def left(real, imag):
        high, low = split_table(jnp.block([[real, -imag], [imag, real]]))
        return jnp.concatenate([high, high, low], 1)

    def right(real, imag):
        high, low = split_table(jnp.block([[real, imag], [-imag, real]]))
        return jnp.concatenate([high, high, low], 0)

    even = wave(2 * half[:, None] * half[None, :])
    odd = wave((2 * half[:, None] + 1) * half[None, :])
    odd_back = wave(half[:, None] * (2 * half[None, :] + 1))
    return left(*even), left(*odd), left(*odd_back), right(*even), right(*odd), right(*odd_back)


def parity(width):
    columns = lax.broadcasted_iota(jnp.int32, (width, width), 1)
    rows = lax.broadcasted_iota(jnp.int32, (width, width), 0)
    source = columns % (width // 2) * 2 + columns // (width // 2)
    return (rows == source).astype(jnp.float32).astype(jnp.bfloat16)


def exact_dot(value, selection):
    high = value.astype(jnp.bfloat16)
    rest = value - high.astype(jnp.float32)
    middle = rest.astype(jnp.bfloat16)
    low = (rest - middle.astype(jnp.float32)).astype(jnp.bfloat16)
    total = jnp.dot(high, selection, preferred_element_type=jnp.float32)
    total = total + jnp.dot(middle, selection, preferred_element_type=jnp.float32)
    return total + jnp.dot(low, selection, preferred_element_type=jnp.float32)


def deal_kernel(flags_ref, x_ref, *refs):
    *edges, o_ref = refs
    pair = 2 * LANES
    selection = parity(pair)
    for block in range(o_ref.shape[2]):
        if block * pair < x_ref.shape[1]:
            value = x_ref[:, block * pair:(block + 1) * pair]
        else:
            value = jnp.concatenate(
                [jnp.where(flags_ref[k] > 0, ref[...], 0.0) for k, ref in zip((1, 0), edges)], 1
            )
        dealt = exact_dot(value, selection)
        height = o_ref.shape[3]
        for j in range(o_ref.shape[0]):
            for p in range(2):
                o_ref[j, p, block] = dealt[j * height:(j + 1) * height, p * LANES:(p + 1) * LANES]


def deal(flags, value, slices, *edges):
    rows, width = value.shape
    blocks = (width + sum(e.shape[1] for e in edges)) // (2 * LANES)
    vmem = pl.BlockSpec(memory_space=pltpu.VMEM)
    return pl.pallas_call(
        deal_kernel,
        in_specs=[pl.BlockSpec(memory_space=pltpu.SMEM)] + [vmem] * (1 + len(edges)),
        out_specs=vmem,
        out_shape=jax.ShapeDtypeStruct((slices, 2, blocks, rows // slices, LANES), jnp.float32),
        name="deal",
    )(flags, value, *edges)


def weave_kernel(flags_ref, *refs):
    *terms, left_ref, right_ref, o_ref = refs
    pair = 2 * LANES
    rows = lax.broadcasted_iota(jnp.int32, (pair, pair), 0)
    columns = lax.broadcasted_iota(jnp.int32, (pair, pair), 1)
    selection = (columns == rows % LANES * 2 + rows // LANES).astype(jnp.float32).astype(jnp.bfloat16)
    lane = lax.broadcasted_iota(jnp.int32, terms[0].shape[3:], 1)
    blocks = o_ref.shape[1] // pair
    for k in range(blocks):
        parts = []
        for p in range(2):
            stacked = []
            for j in range(terms[0].shape[0]):
                value = terms[0][j, p, k]
                for term in terms[1:]:
                    value = value + term[j, p, k]
                if k == 0:
                    value = value + jnp.where((lane < EDGE // 2) & (flags_ref[0] > 0), left_ref[j, p], 0.0)
                if k == blocks - 1:
                    value = value + jnp.where((lane >= LANES - EDGE // 2) & (flags_ref[1] > 0), right_ref[j, p], 0.0)
                stacked.append(value)
            parts.append(jnp.concatenate(stacked, 0))
        o_ref[:, k * pair:(k + 1) * pair] = exact_dot(jnp.concatenate(parts, 1), selection)


def weave(flags, terms, from_left, from_right):
    slices, _, blocks, height, _ = terms[0].shape
    vmem = pl.BlockSpec(memory_space=pltpu.VMEM)
    return pl.pallas_call(
        weave_kernel,
        in_specs=[pl.BlockSpec(memory_space=pltpu.SMEM)] + [vmem] * (2 + len(terms)),
        out_specs=vmem,
        out_shape=jax.ShapeDtypeStruct((slices * height, (blocks - 1) * 2 * LANES), jnp.float32),
        name="weave",
    )(flags, *terms, from_left, from_right)


def kernel(
    rows_ref, columns_ref, count_ref,
    sources_ref, targets_ref, low_ref, high_ref,
    fixed, pieces, outs,
    whole, total, base, ping, pong, first, second, turn, stack_even, stack_odd, wide_even, wide_odd,
    probe_ref, left_even, left_odd, left_odd_back, right_even, right_odd, right_odd_back, sems,
    *, blocks, slices, spans, out_spans,
):
    slot = pl.program_id(0)
    size = low_ref.shape[0]
    half = size // 2
    groups = size // SUB
    height = pieces[0].shape[1]

    lane = lax.broadcasted_iota(jnp.int32, (SUB, LANES), 1)

    layer = 2 * blocks

    def layers(refs_and_rows, span, j):
        piece, ref, start = refs_and_rows
        low, high = j * layer, (j + 1) * layer
        if span.start > low or span.stop < high:
            return []
        rows = pl.ds(pl.multiple_of(start, height), height)
        return [(piece.at[low - span.start:high - span.start], ref.at[low:high, rows, :])]

    def loads(j):
        out = []
        for k, (piece, span) in enumerate(zip(pieces, spans)):
            for source, target in layers((piece, whole, sources_ref[k]), span, j):
                out.append(pltpu.make_async_copy(source, target, sems.at[j]))
        if j == 0:
            out.append(pltpu.make_async_copy(fixed[0], probe_ref, sems.at[j]))
        else:
            factors = (left_even, left_odd, left_odd_back, right_even, right_odd, right_odd_back)
            out += [pltpu.make_async_copy(a, b, sems.at[j]) for a, b in zip(fixed[1:], factors)]
        return out

    def stores(j):
        out = []
        for piece, (index, span) in zip(outs, out_spans):
            for target, source in layers((piece, total, targets_ref[index]), span, j):
                out.append(pltpu.make_async_copy(source, target, sems.at[slices + j]))
        return out

    last = slot == pl.num_programs(0) - 1

    @pl.when(slot == 0)
    def _():
        for j in range(slices):
            for copy in loads(j):
                copy.start()

        def clear(i, carry):
            for k in range(total.shape[0]):
                total[k, pl.ds(pl.multiple_of(i * SUB, SUB), SUB), :] = jnp.zeros((SUB, LANES), jnp.float32)
            return carry
        lax.fori_loop(0, total.shape[1] // SUB, clear, 0)
        for field in (base, ping, pong):
            for part in range(2):
                for p in range(2):
                    field[part, p, :SUB] = jnp.zeros((SUB, LANES), jnp.float32)
                    field[part, p, SUB + size:] = jnp.zeros((SUB, LANES), jnp.float32)
        for copy in loads(0):
            copy.wait()

    def compute(stage):
        start_row = rows_ref[slot]
        start_column = columns_ref[slot]
        sources = []
        for p in range(2):
            column = start_column + p
            at = (column + blocks * 2 * LANES) // 2
            side = lax.rem(column + blocks * 2 * LANES, 2)
            block = lax.rem(at // LANES, blocks)
            after = lax.rem(at // LANES + 1, blocks)
            sources.append((side * blocks + block, side * blocks + after, at % LANES))

        def tile(t):
            return slice(SUB + t * SUB, 2 * SUB + t * SUB)

        def window(t, j):
            rows = pl.ds(start_row + t * SUB, SUB)
            out = []
            for block, after, shift in sources:
                back = lax.rem(LANES - shift, LANES)
                here = pltpu.roll(whole[j * layer + block, rows, :], back, 1)
                there = pltpu.roll(whole[j * layer + after, rows, :], back, 1)
                out.append(jnp.where(lane < LANES - shift, here, there))
            return out

        def phase(t, j):
            out = []
            for value in window(t, j):
                theta = value - 1.0
                z = theta * theta
                c = COS[4]
                s = SIN[4]
                for k in (3, 2, 1, 0):
                    c = c * z + COS[k]
                    s = s * z + SIN[k]
                out.append((c, s * theta))
            return out

        def laplace(ref, part, t):
            even, odd = (ref[part, p, tile(t)] for p in range(2))
            row = SUB + t * SUB
            even_rows = ref[part, 0, row - 1:row + SUB - 1] + ref[part, 0, row + 1:row + SUB + 1]
            odd_rows = ref[part, 1, row - 1:row + SUB - 1] + ref[part, 1, row + 1:row + SUB + 1]
            even_columns = odd + jnp.where(lane == 0, 0.0, pltpu.roll(odd, 1, 1))
            odd_columns = even + jnp.where(lane == LANES - 1, 0.0, pltpu.roll(even, LANES - 1, 1))
            return (even_rows + even_columns) - 4.0 * even, (odd_rows + odd_columns) - 4.0 * odd

        def step(src, dst, factor):
            for t in range(groups):
                lap_re = laplace(src, 0, t)
                lap_im = laplace(src, 1, t)
                for p in range(2):
                    dst[0, p, tile(t)] = base[0, p, tile(t)] - factor * lap_im[p]
                    dst[1, p, tile(t)] = base[1, p, tile(t)] + factor * lap_re[p]

        def propagate():
            step(base, ping, A_PROP / 4)
            step(ping, pong, A_PROP / 3)
            step(pong, ping, A_PROP / 2)
            step(ping, pong, A_PROP)

        def enter(t, j, source, offset, kept):
            for p, (c, s) in enumerate(phase(t, j)):
                re = source[0, p, pl.ds(offset + t * SUB, SUB)]
                im = source[1, p, pl.ds(offset + t * SUB, SUB)]
                new_re, new_im = re * c - im * s, re * s + im * c
                base[0, p, tile(t)] = new_re
                base[1, p, tile(t)] = new_im
                kept[0, p, tile(t)] = new_re
                kept[1, p, tile(t)] = new_im
                if j == slices - 1:
                    turn[0, p, tile(t)] = c
                    turn[1, p, tile(t)] = s

        def leave(tiles, j, kept):
            sums = []
            for t in tiles:
                rows = pl.ds(start_row + t * SUB, SUB)
                for p, (block, after, shift) in enumerate(sources):
                    re = pong[0, p, tile(t)]
                    im = pong[1, p, tile(t)]
                    grad = -(re * kept[1, p, tile(t)] + im * kept[0, p, tile(t)])
                    if j:
                        c = turn[0, p, tile(t)]
                        s = turn[1, p, tile(t)]
                        base[0, p, tile(t)] = re * c - im * s
                        base[1, p, tile(t)] = re * s + im * c
                    rolled = pltpu.roll(grad, shift, 1)
                    here = j * layer + block
                    there = j * layer + after
                    sums.append((here, rows, total[here, rows, :] + jnp.where(lane < shift, 0.0, rolled)))
                    sums.append((there, rows, total[there, rows, :] + jnp.where(lane < shift, rolled, 0.0)))
            for plane, rows, value in sums:
                total[plane, rows, :] = value

        def dot(a, b):
            return jnp.dot(a[...], b[...], preferred_element_type=jnp.float32)

        def put_stack(stack, part, p, value):
            high, low = split(value)
            for k, piece in enumerate((high, low, high)):
                stack[k * size + part * half:k * size + (part + 1) * half, p * LANES:(p + 1) * LANES] = piece

        def put_wide(wide, rows, part, value):
            high, low = split(value)
            for k, piece in enumerate((high, low, high)):
                wide[rows, k * size + part * half:k * size + (part + 1) * half] = piece

        def lanes(k):
            return slice(k * LANES, (k + 1) * LANES)

        if stage == 0:
            for t in range(groups):
                enter(t, 0, probe_ref, 0, first)
            propagate()
            return
        if stage == 2:
            propagate()
            for t in range(0, groups, 8):
                leave(range(t, t + 8), 0, first)
            return
        for t in range(groups):
            enter(t, 1, pong, SUB, second)
        propagate()

        upper, lower = slice(0, half), slice(half, size)
        for part in range(2):
            for p in range(2):
                top = pong[part, p, SUB:SUB + half]
                bottom = pong[part, p, SUB + half:SUB + size]
                put_stack(stack_even, part, p, top + bottom)
                put_stack(stack_odd, part, p, top - bottom)
        for rows, inner in ((upper, dot(left_even, stack_even)), (lower, dot(left_odd, stack_odd))):
            for part, own in enumerate((upper, lower)):
                put_wide(wide_even, rows, part, inner[own, lanes(0)])
                put_wide(wide_odd, rows, part, inner[own, lanes(1)])
        even = dot(wide_even, right_even)
        odd = dot(wide_odd, right_odd)
        for k, rows in enumerate((upper, lower)):
            pulled = []
            for sign, data in ((1, low_ref), (-1, high_ref)):
                far_re = even[rows, lanes(0)] + sign * odd[rows, lanes(0)]
                far_im = even[rows, lanes(1)] + sign * odd[rows, lanes(1)]
                excess = (far_re * far_re + far_im * far_im) - data[pl.ds(k, half, stride=2), :]
                scaled = (4.0 * LOSS_SCALE) * excess
                pulled.append((scaled * far_re, -(scaled * far_im)))
            for part in range(2):
                put_wide(wide_even, rows, part, pulled[0][part] + pulled[1][part])
                put_wide(wide_odd, rows, part, pulled[0][part] - pulled[1][part])
        for p, inner in enumerate((dot(wide_even, right_even), dot(wide_odd, right_odd_back))):
            for part in range(2):
                put_stack(stack_even, part, p, inner[upper, lanes(part)])
                put_stack(stack_odd, part, p, inner[lower, lanes(part)])
        even = dot(left_even, stack_even)
        odd = dot(left_odd_back, stack_odd)
        for part, own in enumerate((upper, lower)):
            for p in range(2):
                base[part, p, SUB:SUB + half] = even[own, lanes(p)] + odd[own, lanes(p)]
                base[part, p, SUB + half:SUB + size] = even[own, lanes(p)] - odd[own, lanes(p)]

        propagate()
        for t in range(0, groups, 8):
            leave(range(t, t + 8), 1, second)

    used = slot < count_ref[0]
    pl.when(used)(lambda: compute(0))

    @pl.when(slot == 0)
    def _():
        for j in range(1, slices):
            for copy in loads(j):
                copy.wait()

    pl.when(used)(lambda: compute(1))

    @pl.when(last)
    def _():
        for j in range(1, slices):
            for copy in stores(j):
                copy.start()

    pl.when(used)(lambda: compute(2))

    @pl.when(last)
    def _():
        for copy in stores(0):
            copy.start()
        for j in range(slices):
            for copy in stores(j):
                copy.wait()


def window_gradients(rows, columns, count, sources, targets, pieces, spans, out_spans, probe, measured, slices, planes, factors):
    slots, size = measured.shape[:2]
    height = pieces[0].shape[1]
    blocks = planes // (2 * slices)
    anywhere = pl.BlockSpec(memory_space=pl.ANY)
    field = pltpu.VMEM((2, 2, size + 2 * SUB, LANES), jnp.float32)
    plane = pltpu.VMEM((planes, targets.shape[0] * height, LANES), jnp.float32)
    tall = pltpu.VMEM((3 * size, size), jnp.bfloat16)
    wide = pltpu.VMEM((size, 3 * size), jnp.bfloat16)
    count_in, count_out = len(pieces), len(out_spans)

    fixed = (probe, *factors)

    def body(*refs):
        head, held, refs = refs[:7], refs[7:7 + len(fixed)], refs[7 + len(fixed):]
        return kernel(
            *head, held, refs[:count_in], refs[count_in:count_in + count_out], *refs[count_in + count_out:],
            blocks=blocks, slices=slices, spans=spans, out_spans=out_spans,
        )

    return pl.pallas_call(
        body,
        grid_spec=pltpu.PrefetchScalarGridSpec(
            num_scalar_prefetch=5,
            grid=(slots,),
            in_specs=[
                pl.BlockSpec((None, size, LANES), lambda k, *_: (k, 0, 0)),
                pl.BlockSpec((None, size, LANES), lambda k, *_: (k, 0, 1)),
                *[anywhere for _ in (*fixed, *pieces)],
            ],
            out_specs=[anywhere] * count_out,
            scratch_shapes=[plane, plane] + [field] * 6 + [tall, tall, wide, wide]
            + [pltpu.VMEM(f.shape, f.dtype) for f in fixed] + [pltpu.SemaphoreType.DMA((2 * slices,))],
        ),
        out_shape=[
            jax.ShapeDtypeStruct((span.stop - span.start, height, LANES), jnp.float32) for _, span in out_spans
        ],
        compiler_params=pltpu.CompilerParams(vmem_limit_bytes=48 * 2**20),
        name="windows",
    )(rows, columns, count, sources, targets, measured, measured, *fixed, *pieces)


def ring_of(slow, fast):
    if slow % 2 and fast % 2 == 0:
        return [y * fast + x for x, y in ((c // slow, c % slow) for c in ring_of(fast, slow))]
    if fast == 1 or slow % 2:
        return list(range(slow * fast))
    path = []
    for z in range(slow):
        row = range(1, fast)
        path += [z * fast + y for y in (row if z % 2 == 0 else reversed(row))]
    return path + [z * fast for z in reversed(range(slow))]


def grid_of(devices):
    count = len(devices)
    cores = len({d.core_on_chip for d in devices})
    chips = [tuple(devices[i].coords) for i in range(0, count, cores)]
    fast = 1
    if len(chips) > 1:
        moving = [a != b for a, b in zip(chips[0], chips[1])]
        while fast < len(chips) and all(m or a == b for m, a, b in zip(moving, chips[0], chips[fast])):
            fast += 1
    if len(chips) % fast:
        fast = 1
    return len(chips) // fast, fast, cores


def shards(potential, probe_wave, offsets, members, counts, measured, *, grid):
    slices, height, own_width = potential.shape
    size = probe_wave.shape[-1]
    strips = lax.axis_size("strip")
    strip = lax.axis_index("strip")
    flags = jnp.stack([strip > 0, strip < strips - 1]).astype(jnp.int32)
    slow, fast, cores = grid
    ring = ring_of(slow, fast)
    chips = len(ring)
    reach = (chips - 1) // 2

    def to_neighbours(rightward, leftward):
        if strips == 2:
            sent = rightward if rightward is leftward else jnp.where(strip == 0, rightward, leftward)
            got = lax.ppermute(sent, "strip", [(0, 1), (1, 0)])
            return got, got
        ahead = [(i, (i + 1) % strips) for i in range(strips)]
        return lax.ppermute(rightward, "strip", ahead), lax.ppermute(leftward, "strip", [(j, i) for i, j in ahead])

    def around(value, by):
        pairs = []
        for k, chip in enumerate(ring):
            for core in range(cores):
                pairs.append((chip * cores + core, ring[(k + by) % chips] * cores + core))
        return lax.ppermute(value, "probe", pairs)

    def inside(value, by):
        if by == 0:
            return value
        pairs = [(chip * cores + c, chip * cores + (c + by) % cores) for chip in range(chips) for c in range(cores)]
        return lax.ppermute(value, "probe", pairs)

    flat = potential.reshape(slices * height, own_width)
    from_left, from_right = to_neighbours(flat[:, own_width - EDGE:], flat[:, :EDGE])
    piece = deal(flags, flat, slices, from_right, from_left)
    piece, probe_wave, offsets, members, zero = lax.optimization_barrier(
        (piece, probe_wave, offsets, members, jnp.zeros((), jnp.int32))
    )
    blocks = piece.shape[2]
    planes = 2 * blocks * slices
    every, upper, lower = slice(0, planes), slice(0, planes // 2), slice(planes // 2, planes)
    piece = piece.reshape(planes, height, LANES)

    order = jnp.array(ring, jnp.int32)
    far = [(chips // 2, upper), (chips // 2, lower)] if chips % 2 == 0 else []
    near = [(s * d, every) for d in range(1, reach + 1) for s in (-1, 1)]
    offsets_in, spans = [], []
    for d, span in [(0, every), *near, *far]:
        for c in range(cores):
            spans.append(span)
            offsets_in.append((d, -c))
    out_spans, offsets_out = [], []
    for d in range(-reach, chips - reach):
        for c in range(cores):
            halves = (upper, lower) if 2 * d == chips else (every,)
            out_spans += [(len(offsets_out), span) for span in halves]
            offsets_out.append((d, c))

    def fields(zero):
        positions = members[0, 0] + zero
        probe = deal(flags, probe_wave.reshape(2 * size, size), 2).reshape(2, 2, size, LANES)
        return offsets[0, 0][positions], offsets[0, 1][positions], probe

    def places(zero):
        me = lax.axis_index("probe") + zero
        seat = jnp.sum(jnp.where(order == me // cores, jnp.arange(chips, dtype=jnp.int32), 0))
        out = []
        for listed in (offsets_in, offsets_out):
            d, c = (jnp.array(v, jnp.int32) for v in zip(*listed))
            chip = jnp.sum(jnp.where(((seat + d + chips) % chips)[:, None] == jnp.arange(chips), order, 0), 1)
            out.append((chip * cores + (me % cores + c + cores) % cores) * height)
        return out

    chores = [fields, lambda zero: tables(size, zero), places]
    done = []

    def beside(zero, *moving):
        if chores and len(done) < len(chores):
            *moving, zero, made = lax.optimization_barrier((*moving, zero, tuple(chores[len(done)](zero))))
            done.append(made)
        return (zero, *moving)

    waiting, pieces = [piece], []

    def share(value):
        pieces.extend(inside(value, c) for c in range(cores))

    ahead = behind = piece
    for d in range(1, reach + 1):
        ahead = around(ahead, 1)
        behind = around(behind, -1)
        zero, ahead, behind = beside(zero, ahead, behind)
        for value in waiting:
            share(lax.optimization_barrier((value, ahead, behind))[0])
        waiting = [ahead, behind]
    if chips % 2 == 0:
        waiting += [around(ahead[upper], 1), around(behind[lower], -1)]
    for value in waiting:
        share(value)
    while len(done) < len(chores):
        beside(zero)
    (rows, columns, probe), factors, (sources, targets) = done
    terms = window_gradients(
        rows, columns, counts[0], sources, targets, pieces, spans, out_spans, probe,
        measured[0, 0], slices, planes, factors,
    )

    by_place = {}
    for (index, span), term in zip(out_spans, terms):
        by_place.setdefault((*offsets_out[index], span.start), term)

    def on_chip(d, start=0):
        own = by_place[d, 0, start]
        for c in range(1, cores):
            own = own + inside(by_place[d, c, start], c)
        return own

    ahead = behind = None
    if chips % 2 == 0:
        ahead = jnp.pad(around(on_chip(chips // 2), 1), ((0, planes // 2), (0, 0), (0, 0)))
        behind = jnp.pad(around(on_chip(chips // 2, planes // 2), -1), ((planes // 2, 0), (0, 0), (0, 0)))
    for d in range(reach, 0, -1):
        front = on_chip(d) if ahead is None else on_chip(d) + ahead
        back = on_chip(-d) if behind is None else on_chip(-d) + behind
        if d > 1:
            ahead, behind = around(front, 1), around(back, -1)
    shape = (slices, 2, blocks, height, LANES)
    own = on_chip(0).reshape(shape)
    mine, edges = [own], own[:, :, -1]
    if reach:
        front, back = front.reshape(shape), back.reshape(shape)
        first = around(front[:, :, -1], 1)
        second = around(back[:, :, -1], -1)
        front, back = front[:, :, :-1], back[:, :, :-1]
        mine += [around(front, 1), around(back, -1)]
        edges = edges + first + second
    elif ahead is not None:
        mine += [ahead.reshape(shape), behind.reshape(shape)]
        edges = sum(term[:, :, -1] for term in mine)
    return weave(flags, mine, *to_neighbours(edges, edges)).reshape(potential.shape)


def solution(mesh):
    placed = (
        P(None, "probe", "strip"),
        P(),
        P("strip", None, None),
        P("strip", "probe", None),
        P("strip", "probe"),
        P("strip", "probe", None, None, None),
    )
    grid = grid_of(list(mesh.devices[:, 0]))
    return jax.shard_map(
        functools.partial(shards, grid=grid), mesh=mesh, in_specs=placed, out_specs=P(None, "probe", "strip"), check_vma=False
    )
```

```python
import functools
import math

import jax
import jax.numpy as jnp
from jax import lax
from jax.experimental import pallas as pl
from jax.experimental.pallas import tpu as pltpu
from jax.sharding import PartitionSpec as P

EDGE = 128
A_PROP = 0.1
LOSS_SCALE = 0.03125
LANES = 128
SUB = 8
COS = (0.9999999993567104, -0.4999999690796125, 0.041666428711172335, -0.0013882473076505886, 2.4093931432702378e-05)
SIN = (0.9999999999413409, -0.1666666638472293, 0.008333311638477454, -0.00019835422091007726, 2.6912728384156356e-06)


def split(value):
    high = value.astype(jnp.bfloat16)
    return high, (value - high.astype(jnp.float32)).astype(jnp.bfloat16)


def split_table(value):
    high = lax.reduce_precision(value, 8, 7)
    return high.astype(jnp.bfloat16), (value - high).astype(jnp.bfloat16)


def tables(size, zero):
    half = jnp.arange(size // 2, dtype=jnp.int32) + zero

    def wave(exponents):
        angles = -2.0 * math.pi / size * (exponents % size).astype(jnp.float32)
        scale = 1.0 / math.sqrt(size)
        return jnp.cos(angles) * scale, jnp.sin(angles) * scale

    def left(real, imag):
        high, low = split_table(jnp.block([[real, -imag], [imag, real]]))
        return jnp.concatenate([high, high, low], 1)

    def right(real, imag):
        high, low = split_table(jnp.block([[real, imag], [-imag, real]]))
        return jnp.concatenate([high, high, low], 0)

    even = wave(2 * half[:, None] * half[None, :])
    odd = wave((2 * half[:, None] + 1) * half[None, :])
    odd_back = wave(half[:, None] * (2 * half[None, :] + 1))
    return left(*even), left(*odd), left(*odd_back), right(*even), right(*odd), right(*odd_back)


def parity(width):
    columns = lax.broadcasted_iota(jnp.int32, (width, width), 1)
    rows = lax.broadcasted_iota(jnp.int32, (width, width), 0)
    source = columns % (width // 2) * 2 + columns // (width // 2)
    return (rows == source).astype(jnp.float32).astype(jnp.bfloat16)


def exact_dot(value, selection):
    high = value.astype(jnp.bfloat16)
    rest = value - high.astype(jnp.float32)
    middle = rest.astype(jnp.bfloat16)
    low = (rest - middle.astype(jnp.float32)).astype(jnp.bfloat16)
    total = jnp.dot(high, selection, preferred_element_type=jnp.float32)
    total = total + jnp.dot(middle, selection, preferred_element_type=jnp.float32)
    return total + jnp.dot(low, selection, preferred_element_type=jnp.float32)


def deal_kernel(flags_ref, x_ref, *refs):
    *edges, o_ref = refs
    pair = 2 * LANES
    selection = parity(pair)
    for block in range(o_ref.shape[2]):
        if block * pair < x_ref.shape[1]:
            value = x_ref[:, block * pair:(block + 1) * pair]
        else:
            value = jnp.concatenate(
                [jnp.where(flags_ref[k] > 0, ref[...], 0.0) for k, ref in zip((1, 0), edges)], 1
            )
        dealt = exact_dot(value, selection)
        height = o_ref.shape[3]
        for j in range(o_ref.shape[0]):
            for p in range(2):
                o_ref[j, p, block] = dealt[j * height:(j + 1) * height, p * LANES:(p + 1) * LANES]


def deal(flags, value, slices, *edges):
    rows, width = value.shape
    blocks = (width + sum(e.shape[1] for e in edges)) // (2 * LANES)
    vmem = pl.BlockSpec(memory_space=pltpu.VMEM)
    return pl.pallas_call(
        deal_kernel,
        in_specs=[pl.BlockSpec(memory_space=pltpu.SMEM)] + [vmem] * (1 + len(edges)),
        out_specs=vmem,
        out_shape=jax.ShapeDtypeStruct((slices, 2, blocks, rows // slices, LANES), jnp.float32),
        name="deal",
    )(flags, value, *edges)


def weave_kernel(slices, flags_ref, *refs):
    *terms, left_ref, right_ref, o_ref = refs
    terms = [terms[k:k + slices] for k in range(0, len(terms), slices)]
    pair = 2 * LANES
    rows = lax.broadcasted_iota(jnp.int32, (pair, pair), 0)
    columns = lax.broadcasted_iota(jnp.int32, (pair, pair), 1)
    selection = (columns == rows % LANES * 2 + rows // LANES).astype(jnp.float32).astype(jnp.bfloat16)
    lane = lax.broadcasted_iota(jnp.int32, terms[0][0].shape[2:], 1)
    blocks = o_ref.shape[1] // pair
    for k in range(blocks):
        parts = []
        for p in range(2):
            stacked = []
            for j in range(slices):
                value = terms[0][j][p, k]
                for term in terms[1:]:
                    value = value + term[j][p, k]
                if k == 0:
                    value = value + jnp.where((lane < EDGE // 2) & (flags_ref[0] > 0), left_ref[j, p], 0.0)
                if k == blocks - 1:
                    value = value + jnp.where((lane >= LANES - EDGE // 2) & (flags_ref[1] > 0), right_ref[j, p], 0.0)
                stacked.append(value)
            parts.append(jnp.concatenate(stacked, 0))
        o_ref[:, k * pair:(k + 1) * pair] = exact_dot(jnp.concatenate(parts, 1), selection)


def weave(flags, terms, from_left, from_right):
    slices = len(terms[0])
    _, blocks, height, _ = terms[0][0].shape
    terms = [part for term in terms for part in term]
    vmem = pl.BlockSpec(memory_space=pltpu.VMEM)
    return pl.pallas_call(
        functools.partial(weave_kernel, slices),
        in_specs=[pl.BlockSpec(memory_space=pltpu.SMEM)] + [vmem] * (2 + len(terms)),
        out_specs=vmem,
        out_shape=jax.ShapeDtypeStruct((slices * height, (blocks - 1) * 2 * LANES), jnp.float32),
        name="weave",
    )(flags, *terms, from_left, from_right)


def kernel(
    rows_ref, columns_ref, count_ref,
    sources_ref, targets_ref, low_ref, high_ref,
    fixed, pieces, outs,
    whole, total, base, ping, pong, first, second, turn, stack_even, stack_odd, wide_even, wide_odd,
    probe_ref, left_even, left_odd, left_odd_back, right_even, right_odd, right_odd_back, sems,
    *, blocks, slices, spans, out_spans,
):
    slot = pl.program_id(0)
    size = low_ref.shape[0]
    half = size // 2
    groups = size // SUB
    height = pieces[0].shape[1]

    lane = lax.broadcasted_iota(jnp.int32, (SUB, LANES), 1)

    layer = 2 * blocks

    def layers(refs_and_rows, span, j):
        piece, ref, start = refs_and_rows
        low, high = j * layer, (j + 1) * layer
        if span.start > low or span.stop < high:
            return []
        rows = pl.ds(pl.multiple_of(start, height), height)
        return [(piece.at[low - span.start:high - span.start], ref.at[low:high, rows, :])]

    def loads(j):
        out = []
        for k, (piece, span) in enumerate(zip(pieces, spans)):
            for source, target in layers((piece, whole, sources_ref[k]), span, j):
                out.append(pltpu.make_async_copy(source, target, sems.at[j]))
        if j == 0:
            out.append(pltpu.make_async_copy(fixed[0], probe_ref, sems.at[j]))
        else:
            factors = (left_even, left_odd, left_odd_back, right_even, right_odd, right_odd_back)
            out += [pltpu.make_async_copy(a, b, sems.at[j]) for a, b in zip(fixed[1:], factors)]
        return out

    def stores(j):
        out = []
        for piece, (index, span) in zip(outs, out_spans):
            for target, source in layers((piece, total, targets_ref[index]), span, j):
                out.append(pltpu.make_async_copy(source, target, sems.at[slices + j]))
        return out

    def sources_of(index):
        out = []
        for p in range(2):
            column = columns_ref[index] + p + blocks * 2 * LANES
            at = column // 2
            block = lax.rem(at // LANES, blocks)
            after = lax.rem(at // LANES + 1, blocks)
            side = lax.rem(column, 2) * blocks
            out.append((side + block, side + after, at % LANES))
        return rows_ref[index], out

    def put_phases(index, j, tiles):
        start_row, sources = sources_of(index)
        held = turn.at[lax.rem(index, 2), j]
        for t in tiles:
            rows = pl.ds(start_row + t * SUB, SUB)
            for p, (block, after, shift) in enumerate(sources):
                back = lax.rem(LANES - shift, LANES)
                here = pltpu.roll(whole[j * layer + block, rows, :], back, 1)
                there = pltpu.roll(whole[j * layer + after, rows, :], back, 1)
                theta = jnp.where(lane < LANES - shift, here, there) - 1.0
                z = theta * theta
                c = COS[4]
                s = SIN[4]
                for k in (3, 2, 1, 0):
                    c = c * z + COS[k]
                    s = s * z + SIN[k]
                held[0, p, t * SUB:(t + 1) * SUB] = c
                held[1, p, t * SUB:(t + 1) * SUB] = s * theta

    last = slot == pl.num_programs(0) - 1

    @pl.when(slot == 0)
    def _():
        for j in range(slices):
            for copy in loads(j):
                copy.start()

        def clear(i, carry):
            for k in range(total.shape[0]):
                total[k, pl.ds(pl.multiple_of(i * SUB, SUB), SUB), :] = jnp.zeros((SUB, LANES), jnp.float32)
            return carry
        lax.fori_loop(0, total.shape[1] // SUB, clear, 0)
        for field in (base, ping, pong):
            for part in range(2):
                for p in range(2):
                    field[part, p, :SUB] = jnp.zeros((SUB, LANES), jnp.float32)
                    field[part, p, SUB + size:] = jnp.zeros((SUB, LANES), jnp.float32)
        for copy in loads(0):
            copy.wait()
        put_phases(slot, 0, range(groups))

    def compute(stage):
        start_row, sources = sources_of(slot)
        phases = turn.at[lax.rem(slot, 2)]
        def tile(t):
            return slice(SUB + t * SUB, 2 * SUB + t * SUB)

        def laplace(ref, part, t):
            even, odd = (ref[part, p, tile(t)] for p in range(2))
            row = SUB + t * SUB
            even_rows = ref[part, 0, row - 1:row + SUB - 1] + ref[part, 0, row + 1:row + SUB + 1]
            odd_rows = ref[part, 1, row - 1:row + SUB - 1] + ref[part, 1, row + 1:row + SUB + 1]
            even_columns = odd + jnp.where(lane == 0, 0.0, pltpu.roll(odd, 1, 1))
            odd_columns = even + jnp.where(lane == LANES - 1, 0.0, pltpu.roll(even, LANES - 1, 1))
            return (even_rows + even_columns) - 4.0 * even, (odd_rows + odd_columns) - 4.0 * odd

        def step(src, dst, factor):
            for t in range(groups):
                lap_re = laplace(src, 0, t)
                lap_im = laplace(src, 1, t)
                for p in range(2):
                    dst[0, p, tile(t)] = base[0, p, tile(t)] - factor * lap_im[p]
                    dst[1, p, tile(t)] = base[1, p, tile(t)] + factor * lap_re[p]

        def propagate():
            step(base, ping, A_PROP / 4)
            step(ping, pong, A_PROP / 3)
            step(pong, ping, A_PROP / 2)
            step(ping, pong, A_PROP)

        def enter(t, j, source, offset, kept):
            for p in range(2):
                c = phases[j, 0, p, t * SUB:(t + 1) * SUB]
                s = phases[j, 1, p, t * SUB:(t + 1) * SUB]
                re = source[0, p, pl.ds(offset + t * SUB, SUB)]
                im = source[1, p, pl.ds(offset + t * SUB, SUB)]
                new_re, new_im = re * c - im * s, re * s + im * c
                base[0, p, tile(t)] = new_re
                base[1, p, tile(t)] = new_im
                kept[0, p, tile(t)] = new_re
                kept[1, p, tile(t)] = new_im

        def leave(tiles, j, kept):
            sums = []
            for t in tiles:
                rows = pl.ds(start_row + t * SUB, SUB)
                for p, (block, after, shift) in enumerate(sources):
                    re = pong[0, p, tile(t)]
                    im = pong[1, p, tile(t)]
                    grad = -(re * kept[1, p, tile(t)] + im * kept[0, p, tile(t)])
                    if j:
                        c = phases[j, 0, p, t * SUB:(t + 1) * SUB]
                        s = phases[j, 1, p, t * SUB:(t + 1) * SUB]
                        base[0, p, tile(t)] = re * c - im * s
                        base[1, p, tile(t)] = re * s + im * c
                    rolled = pltpu.roll(grad, shift, 1)
                    here = j * layer + block
                    there = j * layer + after
                    sums.append((here, rows, total[here, rows, :] + jnp.where(lane < shift, 0.0, rolled)))
                    sums.append((there, rows, total[there, rows, :] + jnp.where(lane < shift, rolled, 0.0)))
            for plane, rows, value in sums:
                total[plane, rows, :] = value

        def dot(a, b):
            return jnp.dot(a[...], b[...], preferred_element_type=jnp.float32)

        def put_stack(stack, part, p, value):
            high, low = split(value)
            for k, piece in enumerate((high, low, high)):
                stack[k * size + part * half:k * size + (part + 1) * half, p * LANES:(p + 1) * LANES] = piece

        def put_wide(wide, rows, part, value):
            high, low = split(value)
            for k, piece in enumerate((high, low, high)):
                wide[rows, k * size + part * half:k * size + (part + 1) * half] = piece

        def lanes(k):
            return slice(k * LANES, (k + 1) * LANES)

        if stage == 0:
            for t in range(groups):
                enter(t, 0, probe_ref, 0, first)
            propagate()
            return
        if stage == 2:
            propagate()
            for t in range(0, groups, 8):
                leave(range(t, t + 8), 0, first)
            return
        for t in range(groups):
            enter(t, 1, pong, SUB, second)
        propagate()

        upper, lower = slice(0, half), slice(half, size)
        for part in range(2):
            for p in range(2):
                top = pong[part, p, SUB:SUB + half]
                bottom = pong[part, p, SUB + half:SUB + size]
                put_stack(stack_even, part, p, top + bottom)
                put_stack(stack_odd, part, p, top - bottom)
        later = jnp.minimum(slot + 1, pl.num_programs(0) - 1)
        quarter = groups // 2
        put_phases(later, 0, range(quarter))
        for rows, inner in ((upper, dot(left_even, stack_even)), (lower, dot(left_odd, stack_odd))):
            for part, own in enumerate((upper, lower)):
                put_wide(wide_even, rows, part, inner[own, lanes(0)])
                put_wide(wide_odd, rows, part, inner[own, lanes(1)])
        put_phases(later, 0, range(quarter, groups))
        even = dot(wide_even, right_even)
        odd = dot(wide_odd, right_odd)
        for k, rows in enumerate((upper, lower)):
            pulled = []
            for sign, data in ((1, low_ref), (-1, high_ref)):
                far_re = even[rows, lanes(0)] + sign * odd[rows, lanes(0)]
                far_im = even[rows, lanes(1)] + sign * odd[rows, lanes(1)]
                excess = (far_re * far_re + far_im * far_im) - data[pl.ds(k, half, stride=2), :]
                scaled = (4.0 * LOSS_SCALE) * excess
                pulled.append((scaled * far_re, -(scaled * far_im)))
            for part in range(2):
                put_wide(wide_even, rows, part, pulled[0][part] + pulled[1][part])
                put_wide(wide_odd, rows, part, pulled[0][part] - pulled[1][part])
        put_phases(later, 1, range(quarter))
        for p, inner in enumerate((dot(wide_even, right_even), dot(wide_odd, right_odd_back))):
            for part in range(2):
                put_stack(stack_even, part, p, inner[upper, lanes(part)])
                put_stack(stack_odd, part, p, inner[lower, lanes(part)])
        put_phases(later, 1, range(quarter, groups))
        even = dot(left_even, stack_even)
        odd = dot(left_odd_back, stack_odd)
        for part, own in enumerate((upper, lower)):
            for p in range(2):
                base[part, p, SUB:SUB + half] = even[own, lanes(p)] + odd[own, lanes(p)]
                base[part, p, SUB + half:SUB + size] = even[own, lanes(p)] - odd[own, lanes(p)]

        propagate()
        for t in range(0, groups, 8):
            leave(range(t, t + 8), 1, second)

    used = slot < count_ref[0]
    pl.when(used)(lambda: compute(0))

    @pl.when(slot == 0)
    def _():
        for j in range(1, slices):
            for copy in loads(j):
                copy.wait()
            put_phases(slot, j, range(groups))

    pl.when(used)(lambda: compute(1))

    @pl.when(last)
    def _():
        for j in range(1, slices):
            for copy in stores(j):
                copy.start()

    pl.when(used)(lambda: compute(2))

    @pl.when(last)
    def _():
        for copy in stores(0):
            copy.start()
        for j in range(slices):
            for copy in stores(j):
                copy.wait()


def window_gradients(rows, columns, count, sources, targets, pieces, spans, out_spans, probe, measured, slices, planes, factors):
    slots, size = measured.shape[:2]
    height = pieces[0].shape[1]
    blocks = planes // (2 * slices)
    anywhere = pl.BlockSpec(memory_space=pl.ANY)
    field = pltpu.VMEM((2, 2, size + 2 * SUB, LANES), jnp.float32)
    plane = pltpu.VMEM((planes, targets.shape[0] * height, LANES), jnp.float32)
    tall = pltpu.VMEM((3 * size, size), jnp.bfloat16)
    wide = pltpu.VMEM((size, 3 * size), jnp.bfloat16)
    count_in, count_out = len(pieces), len(out_spans)

    fixed = (probe, *factors)

    def body(*refs):
        head, held, refs = refs[:7], refs[7:7 + len(fixed)], refs[7 + len(fixed):]
        return kernel(
            *head, held, refs[:count_in], refs[count_in:count_in + count_out], *refs[count_in + count_out:],
            blocks=blocks, slices=slices, spans=spans, out_spans=out_spans,
        )

    return pl.pallas_call(
        body,
        grid_spec=pltpu.PrefetchScalarGridSpec(
            num_scalar_prefetch=5,
            grid=(slots,),
            in_specs=[
                pl.BlockSpec((None, size, LANES), lambda k, *_: (k, 0, 0)),
                pl.BlockSpec((None, size, LANES), lambda k, *_: (k, 0, 1)),
                *[anywhere for _ in (*fixed, *pieces)],
            ],
            out_specs=[anywhere] * count_out,
            scratch_shapes=[plane, plane] + [field] * 5
            + [pltpu.VMEM((2, slices, 2, 2, size, LANES), jnp.float32)] + [tall, tall, wide, wide]
            + [pltpu.VMEM(f.shape, f.dtype) for f in fixed] + [pltpu.SemaphoreType.DMA((2 * slices,))],
        ),
        out_shape=[
            jax.ShapeDtypeStruct((span.stop - span.start, height, LANES), jnp.float32) for _, span in out_spans
        ],
        compiler_params=pltpu.CompilerParams(vmem_limit_bytes=48 * 2**20),
        name="windows",
    )(rows, columns, count, sources, targets, measured, measured, *fixed, *pieces)


def ring_of(slow, fast):
    if slow % 2 and fast % 2 == 0:
        return [y * fast + x for x, y in ((c // slow, c % slow) for c in ring_of(fast, slow))]
    if fast == 1 or slow % 2:
        return list(range(slow * fast))
    path = []
    for z in range(slow):
        row = range(1, fast)
        path += [z * fast + y for y in (row if z % 2 == 0 else reversed(row))]
    return path + [z * fast for z in reversed(range(slow))]


def grid_of(devices):
    count = len(devices)
    cores = len({d.core_on_chip for d in devices})
    chips = [tuple(devices[i].coords) for i in range(0, count, cores)]
    fast = 1
    if len(chips) > 1:
        moving = [a != b for a, b in zip(chips[0], chips[1])]
        while fast < len(chips) and all(m or a == b for m, a, b in zip(moving, chips[0], chips[fast])):
            fast += 1
    if len(chips) % fast:
        fast = 1
    return len(chips) // fast, fast, cores


def shards(potential, probe_wave, offsets, members, counts, measured, *, grid):
    slices, height, own_width = potential.shape
    size = probe_wave.shape[-1]
    strips = lax.axis_size("strip")
    strip = lax.axis_index("strip")
    flags = jnp.stack([strip > 0, strip < strips - 1]).astype(jnp.int32)
    slow, fast, cores = grid
    ring = ring_of(slow, fast)
    chips = len(ring)
    reach = (chips - 1) // 2

    def to_neighbours(rightward, leftward):
        if strips == 2:
            sent = rightward if rightward is leftward else jnp.where(strip == 0, rightward, leftward)
            got = lax.ppermute(sent, "strip", [(0, 1), (1, 0)])
            return got, got
        ahead = [(i, (i + 1) % strips) for i in range(strips)]
        return lax.ppermute(rightward, "strip", ahead), lax.ppermute(leftward, "strip", [(j, i) for i, j in ahead])

    def around(value, by):
        pairs = []
        for k, chip in enumerate(ring):
            for core in range(cores):
                pairs.append((chip * cores + core, ring[(k + by) % chips] * cores + core))
        return lax.ppermute(value, "probe", pairs)

    def inside(value, by):
        if by == 0:
            return value
        pairs = [(chip * cores + c, chip * cores + (c + by) % cores) for chip in range(chips) for c in range(cores)]
        return lax.ppermute(value, "probe", pairs)

    flat = potential.reshape(slices * height, own_width)
    from_left, from_right = to_neighbours(flat[:, own_width - EDGE:], flat[:, :EDGE])
    piece = deal(flags, flat, slices, from_right, from_left)
    piece, probe_wave, offsets, members, zero = lax.optimization_barrier(
        (piece, probe_wave, offsets, members, jnp.zeros((), jnp.int32))
    )
    blocks = piece.shape[2]
    planes = 2 * blocks * slices
    every, upper, lower = slice(0, planes), slice(0, planes // 2), slice(planes // 2, planes)
    piece = piece.reshape(planes, height, LANES)

    order = jnp.array(ring, jnp.int32)
    far = [(chips // 2, upper), (chips // 2, lower)] if chips % 2 == 0 else []
    near = [(s * d, every) for d in range(1, reach + 1) for s in (-1, 1)]
    offsets_in, spans = [], []
    for d, span in [(0, every), *near, *far]:
        for c in range(cores):
            spans.append(span)
            offsets_in.append((d, -c))
    out_spans, offsets_out = [], []
    for d in range(-reach, chips - reach):
        for c in range(cores):
            halves = (upper, lower) if 2 * d == chips else (every,)
            out_spans += [(len(offsets_out), span) for span in halves]
            offsets_out.append((d, c))

    def fields(zero):
        positions = members[0, 0] + zero
        probe = deal(flags, probe_wave.reshape(2 * size, size), 2).reshape(2, 2, size, LANES)
        return offsets[0, 0][positions], offsets[0, 1][positions], probe

    def places(zero):
        me = lax.axis_index("probe") + zero
        seat = jnp.sum(jnp.where(order == me // cores, jnp.arange(chips, dtype=jnp.int32), 0))
        out = []
        for listed in (offsets_in, offsets_out):
            d, c = (jnp.array(v, jnp.int32) for v in zip(*listed))
            chip = jnp.sum(jnp.where(((seat + d + chips) % chips)[:, None] == jnp.arange(chips), order, 0), 1)
            out.append((chip * cores + (me % cores + c + cores) % cores) * height)
        return out

    chores = [fields, lambda zero: tables(size, zero), places]
    done = []

    def beside(zero, *moving):
        if chores and len(done) < len(chores):
            *moving, zero, made = lax.optimization_barrier((*moving, zero, tuple(chores[len(done)](zero))))
            done.append(made)
        return (zero, *moving)

    waiting, pieces = [piece], []

    def share(value):
        pieces.extend(inside(value, c) for c in range(cores))

    ahead = behind = piece
    for d in range(1, reach + 1):
        ahead = around(ahead, 1)
        behind = around(behind, -1)
        zero, ahead, behind = beside(zero, ahead, behind)
        for value in waiting:
            share(lax.optimization_barrier((value, ahead, behind))[0])
        waiting = [ahead, behind]
    if chips % 2 == 0:
        waiting += [around(ahead[upper], 1), around(behind[lower], -1)]
    for value in waiting:
        share(value)
    while len(done) < len(chores):
        beside(zero)
    (rows, columns, probe), factors, (sources, targets) = done
    terms = window_gradients(
        rows, columns, counts[0], sources, targets, pieces, spans, out_spans, probe,
        measured[0, 0], slices, planes, factors,
    )

    by_place = {}
    for (index, span), term in zip(out_spans, terms):
        by_place.setdefault((*offsets_out[index], span.start), term)

    layer = planes // slices
    shape = (2, blocks, height, LANES)
    shared = {
        (d, c, start): inside(term, c) for (d, c, start), term in by_place.items() if c
    }

    def on_chip(d, j):
        start = j * layer if (d, 0, j * layer) in by_place and 2 * d == chips else 0
        cut = slice(j * layer - start, (j + 1) * layer - start)
        own = by_place[d, 0, start][cut]
        for c in range(1, cores):
            own = own + shared[d, c, start][cut]
        return own

    ahead, behind = [None] * slices, [None] * slices
    if chips % 2 == 0:
        for j in range(slices):
            if j < slices // 2:
                ahead[j] = around(on_chip(chips // 2, j), 1)
            else:
                behind[j] = around(on_chip(chips // 2, j), -1)

    def joined(d, j, arrived):
        return on_chip(d, j) if arrived is None else on_chip(d, j) + arrived

    for d in range(reach, 1, -1):
        for j in range(slices):
            front, back = joined(d, j, ahead[j]), joined(-d, j, behind[j])
            ahead[j], behind[j] = around(front, 1), around(back, -1)
    own = [on_chip(0, j).reshape(shape) for j in range(slices)]
    mine = [own]
    edges = jnp.stack([v[:, -1] for v in own])
    if reach:
        front = [joined(1, j, ahead[j]).reshape(shape) for j in range(slices)]
        back = [joined(-1, j, behind[j]).reshape(shape) for j in range(slices)]
        first = around(jnp.stack([v[:, -1] for v in front]), 1)
        second = around(jnp.stack([v[:, -1] for v in back]), -1)
        mine += [[around(v[:, :-1], 1) for v in front], [around(v[:, :-1], -1) for v in back]]
        edges = edges + first + second
    else:
        for last in (ahead, behind):
            some = [jnp.zeros(shape, jnp.float32) if v is None else v.reshape(shape) for v in last]
            mine.append(some)
            edges = edges + jnp.stack([v[:, -1] for v in some])
    return weave(flags, mine, *to_neighbours(edges, edges)).reshape(potential.shape)


def solution(mesh):
    placed = (
        P(None, "probe", "strip"),
        P(),
        P("strip", None, None),
        P("strip", "probe", None),
        P("strip", "probe"),
        P("strip", "probe", None, None, None),
    )
    grid = grid_of(list(mesh.devices[:, 0]))
    return jax.shard_map(
        functools.partial(shards, grid=grid), mesh=mesh, in_specs=placed, out_specs=P(None, "probe", "strip"), check_vma=False
    )
```

```python
import functools
import math

import jax
import jax.numpy as jnp
from jax import lax
from jax.experimental import pallas as pl
from jax.experimental.pallas import tpu as pltpu
from jax.sharding import PartitionSpec as P

EDGE = 128
A_PROP = 0.1
LOSS_SCALE = 0.03125
LANES = 128
SUB = 8
COS = (0.9999999993567104, -0.4999999690796125, 0.041666428711172335, -0.0013882473076505886, 2.4093931432702378e-05)
SIN = (0.9999999999413409, -0.1666666638472293, 0.008333311638477454, -0.00019835422091007726, 2.6912728384156356e-06)


def split(value):
    high = value.astype(jnp.bfloat16)
    return high, (value - high.astype(jnp.float32)).astype(jnp.bfloat16)


def split_table(value):
    high = lax.reduce_precision(value, 8, 7)
    return high.astype(jnp.bfloat16), (value - high).astype(jnp.bfloat16)


def tables(size, zero):
    half = jnp.arange(size // 2, dtype=jnp.int32) + zero

    def wave(exponents):
        angles = -2.0 * math.pi / size * (exponents % size).astype(jnp.float32)
        scale = 1.0 / math.sqrt(size)
        return jnp.cos(angles) * scale, jnp.sin(angles) * scale

    def left(real, imag):
        high, low = split_table(jnp.block([[real, -imag], [imag, real]]))
        return jnp.concatenate([high, high, low], 1)

    def right(real, imag):
        high, low = split_table(jnp.block([[real, imag], [-imag, real]]))
        return jnp.concatenate([high, high, low], 0)

    even = wave(2 * half[:, None] * half[None, :])
    odd = wave((2 * half[:, None] + 1) * half[None, :])
    odd_back = wave(half[:, None] * (2 * half[None, :] + 1))
    return left(*even), left(*odd), left(*odd_back), right(*even), right(*odd), right(*odd_back)


def parity(width):
    columns = lax.broadcasted_iota(jnp.int32, (width, width), 1)
    rows = lax.broadcasted_iota(jnp.int32, (width, width), 0)
    source = columns % (width // 2) * 2 + columns // (width // 2)
    return (rows == source).astype(jnp.float32).astype(jnp.bfloat16)


def exact_dot(value, selection):
    high = value.astype(jnp.bfloat16)
    rest = value - high.astype(jnp.float32)
    middle = rest.astype(jnp.bfloat16)
    low = (rest - middle.astype(jnp.float32)).astype(jnp.bfloat16)
    total = jnp.dot(high, selection, preferred_element_type=jnp.float32)
    total = total + jnp.dot(middle, selection, preferred_element_type=jnp.float32)
    return total + jnp.dot(low, selection, preferred_element_type=jnp.float32)


def deal_kernel(flags_ref, x_ref, *refs):
    *edges, o_ref = refs
    pair = 2 * LANES
    selection = parity(pair)
    for block in range(o_ref.shape[2]):
        if block * pair < x_ref.shape[1]:
            value = x_ref[:, block * pair:(block + 1) * pair]
        else:
            value = jnp.concatenate(
                [jnp.where(flags_ref[k] > 0, ref[...], 0.0) for k, ref in zip((1, 0), edges)], 1
            )
        dealt = exact_dot(value, selection)
        height = o_ref.shape[3]
        for j in range(o_ref.shape[0]):
            for p in range(2):
                o_ref[j, p, block] = dealt[j * height:(j + 1) * height, p * LANES:(p + 1) * LANES]


def deal(flags, value, slices, *edges):
    rows, width = value.shape
    blocks = (width + sum(e.shape[1] for e in edges)) // (2 * LANES)
    vmem = pl.BlockSpec(memory_space=pltpu.VMEM)
    return pl.pallas_call(
        deal_kernel,
        in_specs=[pl.BlockSpec(memory_space=pltpu.SMEM)] + [vmem] * (1 + len(edges)),
        out_specs=vmem,
        out_shape=jax.ShapeDtypeStruct((slices, 2, blocks, rows // slices, LANES), jnp.float32),
        name="deal",
    )(flags, value, *edges)


def weave_kernel(slices, flags_ref, *refs):
    *terms, left_ref, right_ref, o_ref = refs
    terms = [terms[k:k + slices] for k in range(0, len(terms), slices)]
    pair = 2 * LANES
    rows = lax.broadcasted_iota(jnp.int32, (pair, pair), 0)
    columns = lax.broadcasted_iota(jnp.int32, (pair, pair), 1)
    selection = (columns == rows % LANES * 2 + rows // LANES).astype(jnp.float32).astype(jnp.bfloat16)
    lane = lax.broadcasted_iota(jnp.int32, terms[0][0].shape[2:], 1)
    blocks = o_ref.shape[1] // pair
    for k in range(blocks):
        parts = []
        for p in range(2):
            stacked = []
            for j in range(slices):
                value = terms[0][j][p, k]
                for term in terms[1:]:
                    value = value + term[j][p, k]
                if k == 0:
                    value = value + jnp.where((lane < EDGE // 2) & (flags_ref[0] > 0), left_ref[j, p], 0.0)
                if k == blocks - 1:
                    value = value + jnp.where((lane >= LANES - EDGE // 2) & (flags_ref[1] > 0), right_ref[j, p], 0.0)
                stacked.append(value)
            parts.append(jnp.concatenate(stacked, 0))
        o_ref[:, k * pair:(k + 1) * pair] = exact_dot(jnp.concatenate(parts, 1), selection)


def weave(flags, terms, from_left, from_right):
    slices = len(terms[0])
    _, blocks, height, _ = terms[0][0].shape
    terms = [part for term in terms for part in term]
    vmem = pl.BlockSpec(memory_space=pltpu.VMEM)
    return pl.pallas_call(
        functools.partial(weave_kernel, slices),
        in_specs=[pl.BlockSpec(memory_space=pltpu.SMEM)] + [vmem] * (2 + len(terms)),
        out_specs=vmem,
        out_shape=jax.ShapeDtypeStruct((slices * height, (blocks - 1) * 2 * LANES), jnp.float32),
        name="weave",
    )(flags, *terms, from_left, from_right)


def kernel(
    rows_ref, columns_ref, count_ref,
    sources_ref, targets_ref, low_ref, high_ref,
    fixed, pieces, outs,
    whole, total, base, ping, pong, first, second, turn, stack_even, stack_odd, wide_even, wide_odd,
    probe_ref, left_even, left_odd, left_odd_back, right_even, right_odd, right_odd_back, sems,
    *, blocks, slices, spans, out_spans,
):
    slot = pl.program_id(0)
    size = low_ref.shape[0]
    half = size // 2
    groups = size // SUB
    height = pieces[0].shape[1]

    lane = lax.broadcasted_iota(jnp.int32, (SUB, LANES), 1)

    layer = 2 * blocks

    def layers(refs_and_rows, span, j):
        piece, ref, start = refs_and_rows
        low, high = j * layer, (j + 1) * layer
        if span.start > low or span.stop < high:
            return []
        rows = pl.ds(pl.multiple_of(start, height), height)
        return [(piece.at[low - span.start:high - span.start], ref.at[low:high, rows, :])]

    def loads(j):
        out = []
        for k, (piece, span) in enumerate(zip(pieces, spans)):
            for source, target in layers((piece, whole, sources_ref[k]), span, j):
                out.append(pltpu.make_async_copy(source, target, sems.at[j]))
        if j == 0:
            out.append(pltpu.make_async_copy(fixed[0], probe_ref, sems.at[j]))
        else:
            factors = (left_even, left_odd, left_odd_back, right_even, right_odd, right_odd_back)
            out += [pltpu.make_async_copy(a, b, sems.at[j]) for a, b in zip(fixed[1:], factors)]
        return out

    def stores(j):
        out = []
        for piece, (index, span) in zip(outs, out_spans):
            for target, source in layers((piece, total, targets_ref[index]), span, j):
                out.append(pltpu.make_async_copy(source, target, sems.at[slices + j]))
        return out

    def sources_of(index):
        out = []
        for p in range(2):
            column = columns_ref[index] + p + blocks * 2 * LANES
            at = column // 2
            block = lax.rem(at // LANES, blocks)
            after = lax.rem(at // LANES + 1, blocks)
            side = lax.rem(column, 2) * blocks
            out.append((side + block, side + after, at % LANES))
        return rows_ref[index], out

    def put_phases(index, j, tiles):
        start_row, sources = sources_of(index)
        held = turn.at[lax.rem(index, 2), j]
        for t in tiles:
            rows = pl.ds(start_row + t * SUB, SUB)
            for p, (block, after, shift) in enumerate(sources):
                back = lax.rem(LANES - shift, LANES)
                here = pltpu.roll(whole[j * layer + block, rows, :], back, 1)
                there = pltpu.roll(whole[j * layer + after, rows, :], back, 1)
                theta = jnp.where(lane < LANES - shift, here, there) - 1.0
                z = theta * theta
                c = COS[4]
                s = SIN[4]
                for k in (3, 2, 1, 0):
                    c = c * z + COS[k]
                    s = s * z + SIN[k]
                held[0, p, t * SUB:(t + 1) * SUB] = c
                held[1, p, t * SUB:(t + 1) * SUB] = s * theta

    last = slot == pl.num_programs(0) - 1

    @pl.when(slot == 0)
    def _():
        for j in range(slices):
            for copy in loads(j):
                copy.start()

        def clear(i, carry):
            for k in range(total.shape[0]):
                total[k, pl.ds(pl.multiple_of(i * SUB, SUB), SUB), :] = jnp.zeros((SUB, LANES), jnp.float32)
            return carry
        lax.fori_loop(0, total.shape[1] // SUB, clear, 0)
        for field in (base, ping, pong):
            for part in range(2):
                for p in range(2):
                    field[part, p, :SUB] = jnp.zeros((SUB, LANES), jnp.float32)
                    field[part, p, SUB + size:] = jnp.zeros((SUB, LANES), jnp.float32)
        for copy in loads(0):
            copy.wait()
        put_phases(slot, 0, range(groups))

    def compute(stage):
        start_row, sources = sources_of(slot)
        phases = turn.at[lax.rem(slot, 2)]
        def tile(t):
            return slice(SUB + t * SUB, 2 * SUB + t * SUB)

        def laplace(ref, part, t):
            even, odd = (ref[part, p, tile(t)] for p in range(2))
            row = SUB + t * SUB
            even_rows = ref[part, 0, row - 1:row + SUB - 1] + ref[part, 0, row + 1:row + SUB + 1]
            odd_rows = ref[part, 1, row - 1:row + SUB - 1] + ref[part, 1, row + 1:row + SUB + 1]
            even_columns = odd + jnp.where(lane == 0, 0.0, pltpu.roll(odd, 1, 1))
            odd_columns = even + jnp.where(lane == LANES - 1, 0.0, pltpu.roll(even, LANES - 1, 1))
            return (even_rows + even_columns) - 4.0 * even, (odd_rows + odd_columns) - 4.0 * odd

        def step(src, dst, factor):
            for t in range(groups):
                lap_re = laplace(src, 0, t)
                lap_im = laplace(src, 1, t)
                for p in range(2):
                    dst[0, p, tile(t)] = base[0, p, tile(t)] - factor * lap_im[p]
                    dst[1, p, tile(t)] = base[1, p, tile(t)] + factor * lap_re[p]

        def propagate():
            step(base, ping, A_PROP / 4)
            step(ping, pong, A_PROP / 3)
            step(pong, ping, A_PROP / 2)
            step(ping, pong, A_PROP)

        def enter(t, j, source, offset, kept):
            for p in range(2):
                c = phases[j, 0, p, t * SUB:(t + 1) * SUB]
                s = phases[j, 1, p, t * SUB:(t + 1) * SUB]
                re = source[0, p, pl.ds(offset + t * SUB, SUB)]
                im = source[1, p, pl.ds(offset + t * SUB, SUB)]
                new_re, new_im = re * c - im * s, re * s + im * c
                base[0, p, tile(t)] = new_re
                base[1, p, tile(t)] = new_im
                kept[0, p, tile(t)] = new_re
                kept[1, p, tile(t)] = new_im

        def leave(tiles, j, kept):
            sums = []
            for t in tiles:
                rows = pl.ds(start_row + t * SUB, SUB)
                for p, (block, after, shift) in enumerate(sources):
                    re = pong[0, p, tile(t)]
                    im = pong[1, p, tile(t)]
                    grad = -(re * kept[1, p, tile(t)] + im * kept[0, p, tile(t)])
                    if j:
                        c = phases[j, 0, p, t * SUB:(t + 1) * SUB]
                        s = phases[j, 1, p, t * SUB:(t + 1) * SUB]
                        base[0, p, tile(t)] = re * c - im * s
                        base[1, p, tile(t)] = re * s + im * c
                    rolled = pltpu.roll(grad, shift, 1)
                    here = j * layer + block
                    there = j * layer + after
                    sums.append((here, rows, total[here, rows, :] + jnp.where(lane < shift, 0.0, rolled)))
                    sums.append((there, rows, total[there, rows, :] + jnp.where(lane < shift, rolled, 0.0)))
            for plane, rows, value in sums:
                total[plane, rows, :] = value

        def dot(a, b):
            return jnp.dot(a[...], b[...], preferred_element_type=jnp.float32)

        def put_stack(stack, part, p, value):
            high, low = split(value)
            for k, piece in enumerate((high, low, high)):
                stack[k * size + part * half:k * size + (part + 1) * half, p * LANES:(p + 1) * LANES] = piece

        def put_wide(wide, rows, part, value):
            high, low = split(value)
            for k, piece in enumerate((high, low, high)):
                wide[rows, k * size + part * half:k * size + (part + 1) * half] = piece

        def lanes(k):
            return slice(k * LANES, (k + 1) * LANES)

        if stage == 0:
            for t in range(groups):
                enter(t, 0, probe_ref, 0, first)
            propagate()
            return
        if stage == 2:
            propagate()
            for t in range(0, groups, 8):
                leave(range(t, t + 8), 0, first)
            return
        for t in range(groups):
            enter(t, 1, pong, SUB, second)
        propagate()

        upper, lower = slice(0, half), slice(half, size)
        for part in range(2):
            for p in range(2):
                top = pong[part, p, SUB:SUB + half]
                bottom = pong[part, p, SUB + half:SUB + size]
                put_stack(stack_even, part, p, top + bottom)
                put_stack(stack_odd, part, p, top - bottom)
        later = jnp.minimum(slot + 1, pl.num_programs(0) - 1)
        quarter = groups // 2
        put_phases(later, 0, range(quarter))
        for rows, inner in ((upper, dot(left_even, stack_even)), (lower, dot(left_odd, stack_odd))):
            for part, own in enumerate((upper, lower)):
                put_wide(wide_even, rows, part, inner[own, lanes(0)])
                put_wide(wide_odd, rows, part, inner[own, lanes(1)])
        put_phases(later, 0, range(quarter, groups))
        even = dot(wide_even, right_even)
        odd = dot(wide_odd, right_odd)
        for k, rows in enumerate((upper, lower)):
            pulled = []
            for sign, data in ((1, low_ref), (-1, high_ref)):
                far_re = even[rows, lanes(0)] + sign * odd[rows, lanes(0)]
                far_im = even[rows, lanes(1)] + sign * odd[rows, lanes(1)]
                excess = (far_re * far_re + far_im * far_im) - data[pl.ds(k, half, stride=2), :]
                scaled = (4.0 * LOSS_SCALE) * excess
                pulled.append((scaled * far_re, -(scaled * far_im)))
            for part in range(2):
                put_wide(wide_even, rows, part, pulled[0][part] + pulled[1][part])
                put_wide(wide_odd, rows, part, pulled[0][part] - pulled[1][part])
        put_phases(later, 1, range(quarter))
        for p, inner in enumerate((dot(wide_even, right_even), dot(wide_odd, right_odd_back))):
            for part in range(2):
                put_stack(stack_even, part, p, inner[upper, lanes(part)])
                put_stack(stack_odd, part, p, inner[lower, lanes(part)])
        put_phases(later, 1, range(quarter, groups))
        even = dot(left_even, stack_even)
        odd = dot(left_odd_back, stack_odd)
        for part, own in enumerate((upper, lower)):
            for p in range(2):
                base[part, p, SUB:SUB + half] = even[own, lanes(p)] + odd[own, lanes(p)]
                base[part, p, SUB + half:SUB + size] = even[own, lanes(p)] - odd[own, lanes(p)]

        propagate()
        for t in range(0, groups, 8):
            leave(range(t, t + 8), 1, second)

    used = slot < count_ref[0]
    pl.when(used)(lambda: compute(0))

    @pl.when(slot == 0)
    def _():
        for j in range(1, slices):
            for copy in loads(j):
                copy.wait()
            put_phases(slot, j, range(groups))

    pl.when(used)(lambda: compute(1))

    @pl.when(last)
    def _():
        for j in range(1, slices):
            for copy in stores(j):
                copy.start()

    pl.when(used)(lambda: compute(2))

    @pl.when(last)
    def _():
        for copy in stores(0):
            copy.start()
        for j in range(slices):
            for copy in stores(j):
                copy.wait()


def window_gradients(rows, columns, count, sources, targets, pieces, spans, out_spans, probe, measured, slices, planes, factors):
    slots, size = measured.shape[:2]
    height = pieces[0].shape[1]
    blocks = planes // (2 * slices)
    anywhere = pl.BlockSpec(memory_space=pl.ANY)
    field = pltpu.VMEM((2, 2, size + 2 * SUB, LANES), jnp.float32)
    plane = pltpu.VMEM((planes, targets.shape[0] * height, LANES), jnp.float32)
    tall = pltpu.VMEM((3 * size, size), jnp.bfloat16)
    wide = pltpu.VMEM((size, 3 * size), jnp.bfloat16)
    count_in, count_out = len(pieces), len(out_spans)

    fixed = (probe, *factors)

    def body(*refs):
        head, held, refs = refs[:7], refs[7:7 + len(fixed)], refs[7 + len(fixed):]
        return kernel(
            *head, held, refs[:count_in], refs[count_in:count_in + count_out], *refs[count_in + count_out:],
            blocks=blocks, slices=slices, spans=spans, out_spans=out_spans,
        )

    return pl.pallas_call(
        body,
        grid_spec=pltpu.PrefetchScalarGridSpec(
            num_scalar_prefetch=5,
            grid=(slots,),
            in_specs=[
                pl.BlockSpec((None, size, LANES), lambda k, *_: (k, 0, 0)),
                pl.BlockSpec((None, size, LANES), lambda k, *_: (k, 0, 1)),
                *[anywhere for _ in (*fixed, *pieces)],
            ],
            out_specs=[anywhere] * count_out,
            scratch_shapes=[plane, plane] + [field] * 5
            + [pltpu.VMEM((2, slices, 2, 2, size, LANES), jnp.float32)] + [tall, tall, wide, wide]
            + [pltpu.VMEM(f.shape, f.dtype) for f in fixed] + [pltpu.SemaphoreType.DMA((2 * slices,))],
        ),
        out_shape=[
            jax.ShapeDtypeStruct((span.stop - span.start, height, LANES), jnp.float32) for _, span in out_spans
        ],
        compiler_params=pltpu.CompilerParams(vmem_limit_bytes=48 * 2**20),
        name="windows",
    )(rows, columns, count, sources, targets, measured, measured, *fixed, *pieces)


def ring_of(slow, fast):
    if slow % 2 and fast % 2 == 0:
        return [y * fast + x for x, y in ((c // slow, c % slow) for c in ring_of(fast, slow))]
    if fast == 1 or slow % 2:
        return list(range(slow * fast))
    path = []
    for z in range(slow):
        row = range(1, fast)
        path += [z * fast + y for y in (row if z % 2 == 0 else reversed(row))]
    return path + [z * fast for z in reversed(range(slow))]


def grid_of(devices):
    count = len(devices)
    cores = len({d.core_on_chip for d in devices})
    chips = [tuple(devices[i].coords) for i in range(0, count, cores)]
    fast = 1
    if len(chips) > 1:
        moving = [a != b for a, b in zip(chips[0], chips[1])]
        while fast < len(chips) and all(m or a == b for m, a, b in zip(moving, chips[0], chips[fast])):
            fast += 1
    if len(chips) % fast:
        fast = 1
    return len(chips) // fast, fast, cores


def shards(potential, probe_wave, offsets, members, counts, measured, *, grid):
    slices, height, own_width = potential.shape
    size = probe_wave.shape[-1]
    strips = lax.axis_size("strip")
    strip = lax.axis_index("strip")
    flags = jnp.stack([strip > 0, strip < strips - 1]).astype(jnp.int32)
    slow, fast, cores = grid
    ring = ring_of(slow, fast)
    chips = len(ring)
    reach = (chips - 1) // 2

    def to_neighbours(rightward, leftward):
        if strips == 2:
            sent = rightward if rightward is leftward else jnp.where(strip == 0, rightward, leftward)
            got = lax.ppermute(sent, "strip", [(0, 1), (1, 0)])
            return got, got
        ahead = [(i, (i + 1) % strips) for i in range(strips)]
        return lax.ppermute(rightward, "strip", ahead), lax.ppermute(leftward, "strip", [(j, i) for i, j in ahead])

    def around(value, by):
        pairs = []
        for k, chip in enumerate(ring):
            for core in range(cores):
                pairs.append((chip * cores + core, ring[(k + by) % chips] * cores + core))
        return lax.ppermute(value, "probe", pairs)

    def inside(value, by):
        if by == 0:
            return value
        pairs = [(chip * cores + c, chip * cores + (c + by) % cores) for chip in range(chips) for c in range(cores)]
        return lax.ppermute(value, "probe", pairs)

    flat = potential.reshape(slices * height, own_width)
    from_left, from_right = to_neighbours(flat[:, own_width - EDGE:], flat[:, :EDGE])
    piece = deal(flags, flat, slices, from_right, from_left)
    piece, probe_wave, offsets, members, zero = lax.optimization_barrier(
        (piece, probe_wave, offsets, members, jnp.zeros((), jnp.int32))
    )
    blocks = piece.shape[2]
    planes = 2 * blocks * slices
    every, upper, lower = slice(0, planes), slice(0, planes // 2), slice(planes // 2, planes)
    piece = piece.reshape(planes, height, LANES)

    order = jnp.array(ring, jnp.int32)
    far = [(chips // 2, upper), (chips // 2, lower)] if chips % 2 == 0 else []
    near = [(s * d, every) for d in range(1, reach + 1) for s in (-1, 1)]
    offsets_in, spans = [], []
    for d, span in [(0, every), *near, *far]:
        for c in range(cores):
            spans.append(span)
            offsets_in.append((d, -c))
    out_spans, offsets_out = [], []
    for d in range(-reach, chips - reach):
        for c in range(cores):
            halves = (upper, lower) if 2 * d == chips else (every,)
            out_spans += [(len(offsets_out), span) for span in halves]
            offsets_out.append((d, c))

    def fields(zero):
        positions = members[0, 0] + zero
        probe = deal(flags, probe_wave.reshape(2 * size, size), 2).reshape(2, 2, size, LANES)
        return offsets[0, 0][positions], offsets[0, 1][positions], probe

    def places(zero):
        me = lax.axis_index("probe") + zero
        seat = jnp.sum(jnp.where(order == me // cores, jnp.arange(chips, dtype=jnp.int32), 0))
        out = []
        for listed in (offsets_in, offsets_out):
            d, c = (jnp.array(v, jnp.int32) for v in zip(*listed))
            chip = jnp.sum(jnp.where(((seat + d + chips) % chips)[:, None] == jnp.arange(chips), order, 0), 1)
            out.append((chip * cores + (me % cores + c + cores) % cores) * height)
        return out

    chores = [fields, lambda zero: tables(size, zero), places]
    done = []

    def beside(zero, *moving):
        if chores and len(done) < len(chores):
            *moving, zero, made = lax.optimization_barrier((*moving, zero, tuple(chores[len(done)](zero))))
            done.append(made)
        return (zero, *moving)

    waiting, pieces = [piece], []

    def share(value):
        pieces.extend(inside(value, c) for c in range(cores))

    ahead = behind = piece
    for d in range(1, reach + 1):
        ahead = around(ahead, 1)
        behind = around(behind, -1)
        zero, ahead, behind = beside(zero, ahead, behind)
        for value in waiting:
            share(lax.optimization_barrier((value, ahead, behind))[0])
        waiting = [ahead, behind]
    if chips % 2 == 0:
        waiting += [around(ahead[upper], 1), around(behind[lower], -1)]
    for value in waiting:
        share(value)
    while len(done) < len(chores):
        beside(zero)
    (rows, columns, probe), factors, (sources, targets) = done
    terms = window_gradients(
        rows, columns, counts[0], sources, targets, pieces, spans, out_spans, probe,
        measured[0, 0], slices, planes, factors,
    )

    by_place = {}
    for (index, span), term in zip(out_spans, terms):
        by_place.setdefault((*offsets_out[index], span.start), term)

    layer = planes // slices
    shape = (2, blocks, height, LANES)
    shared = {key: inside(term, key[1]) for key, term in by_place.items() if key[1] and 2 * key[0] == chips}
    leading = tuple(shared.values())
    for key, term in by_place.items():
        if key[1] and key not in shared:
            shared[key] = inside(lax.optimization_barrier((term, *leading))[0], key[1])

    def on_chip(d, j):
        start = j * layer if (d, 0, j * layer) in by_place and 2 * d == chips else 0
        cut = slice(j * layer - start, (j + 1) * layer - start)
        own = by_place[d, 0, start][cut]
        for c in range(1, cores):
            own = own + shared[d, c, start][cut]
        return own

    ahead, behind = [None] * slices, [None] * slices
    if chips % 2 == 0:
        for j in range(slices):
            if j < slices // 2:
                ahead[j] = around(on_chip(chips // 2, j), 1)
            else:
                behind[j] = around(on_chip(chips // 2, j), -1)

    def joined(d, j, arrived):
        return on_chip(d, j) if arrived is None else on_chip(d, j) + arrived

    for d in range(reach, 1, -1):
        for j in range(slices):
            front, back = joined(d, j, ahead[j]), joined(-d, j, behind[j])
            ahead[j], behind[j] = around(front, 1), around(back, -1)
    own = [on_chip(0, j).reshape(shape) for j in range(slices)]
    mine = [own]
    edges = jnp.stack([v[:, -1] for v in own])
    if reach:
        front = [joined(1, j, ahead[j]).reshape(shape) for j in range(slices)]
        back = [joined(-1, j, behind[j]).reshape(shape) for j in range(slices)]
        first = around(jnp.stack([v[:, -1] for v in front]), 1)
        second = around(jnp.stack([v[:, -1] for v in back]), -1)
        mine += [[around(v[:, :-1], 1) for v in front], [around(v[:, :-1], -1) for v in back]]
        edges = edges + first + second
    else:
        for last in (ahead, behind):
            some = [jnp.zeros(shape, jnp.float32) if v is None else v.reshape(shape) for v in last]
            mine.append(some)
            edges = edges + jnp.stack([v[:, -1] for v in some])
    return weave(flags, mine, *to_neighbours(edges, edges)).reshape(potential.shape)


def solution(mesh):
    placed = (
        P(None, "probe", "strip"),
        P(),
        P("strip", None, None),
        P("strip", "probe", None),
        P("strip", "probe"),
        P("strip", "probe", None, None, None),
    )
    grid = grid_of(list(mesh.devices[:, 0]))
    return jax.shard_map(
        functools.partial(shards, grid=grid), mesh=mesh, in_specs=placed, out_specs=P(None, "probe", "strip"), check_vma=False
    )
```
